256 devices in a mesh: ctx: 128 (over x_lo, z, y, core), section: 2 (over x_hi).
Axes of the slice: x: 4 (x_hi: 2, x_lo: 2; x = x_hi * 2 + x_lo), y: 4, z: 8, core: 2. Of those that a mesh axis runs over, the one named last changes fastest.
Arguments:
- queries: bfloat16 [32768, 5120], P('ctx', 'section'), as said below
- key_states: bfloat16 [32768, 5120], P('ctx', 'section'), as said below
- value_states: bfloat16 [32768, 5120], P('ctx', 'section'), may hold values from -6 to 6
- out_grad: bfloat16 [32768, 5120], P('ctx', 'section'), may hold values from -6 to 6
- tile_mask: int32 [256, 6], replicated, may hold values from 0 to 1, as said below
Outputs:
- query_grad: bfloat16 [32768, 5120], P(('ctx', 'section'))
- key_grad: bfloat16 [32768, 5120], P(('ctx', 'section'))
- value_grad: bfloat16 [32768, 5120], P(('ctx', 'section'))
The draws below stay inside these ranges and needn't reach their ends.
Inputs may be any that keep to these rules, and one draw needn't show every extreme that they name: tile_mask[t, 2 + (t mod 2)] is 1 for every tile t: each tile attends to itself. `queries`: entries lie within -6 and 6. `key_states`: entries lie within -6 and 6.
All inputs are finite; a program needn't handle non-finite values.
Results may differ from the reference program's by a relative error of at most 0.0096.
Values may be sent and summed in bfloat16 or wider, within the bound.
No kernel may reach another device: no remote copies, remote signals or barrier semaphores. Data moves between devices by JAX's collectives and lax.ppermute only.
A program may use at most 128 MiB of HBM per device.

```python
import math
import jax
import jax.numpy as jnp
from jax import lax

HEAD = 128
TILE = 128
TPD = 2
HEADS = 40
TOKENS = 32768
NT = 256
N_CTX = 128


def draw_queries(key, part):
    own_key = jax.random.fold_in(key, 1)
    entries = jnp.clip(jax.random.normal(own_key, (TOKENS, HEADS * HEAD), jnp.float32), -6.0, 6.0)
    return entries.astype(jnp.bfloat16)


def draw_key_states(key, part):
    own_key = jax.random.fold_in(key, 2)
    entries = jnp.clip(jax.random.normal(own_key, (TOKENS, HEADS * HEAD), jnp.float32), -6.0, 6.0)
    return entries.astype(jnp.bfloat16)


def draw_tile_mask(key, part):
    first, second = jax.random.split(jax.random.fold_in(key, 3))
    level = jax.random.randint(first, (NT, 1), 1, 5)
    random_bits = jax.random.randint(second, (NT, 3 * TPD), 0, 4)
    live_bits = (random_bits < level).astype(jnp.int32)
    column = lax.broadcasted_iota(jnp.int32, (NT, 3 * TPD), 1)
    tile_number = lax.broadcasted_iota(jnp.int32, (NT, 3 * TPD), 0)
    own_tile = (column == TPD + tile_number % TPD).astype(jnp.int32)
    return jnp.maximum(live_bits, own_tile)


def shard_levels(stream_key, dims, cuts, smallest, high):
    factor_of = 1.0
    for position, parts in cuts:
        heights = jax.random.uniform(jax.random.fold_in(jax.random.fold_in(stream_key, 6), position), (parts,), jnp.float32, smallest / len(cuts), high / len(cuts))
        factor_of = factor_of * jnp.repeat(jnp.exp(heights), dims[position] // parts).reshape((-1,) + (1,) * (len(dims) - 1 - position))
    return factor_of


def normal_values(stream_key, dims, spread, bound, cuts=(), held_as=jnp.bfloat16):
    drawn = jax.random.normal(stream_key, dims, jnp.float32) * spread
    if len(cuts) > 0:
        drawn = shard_levels(stream_key, dims, cuts, -0.22, 0.18) * drawn
    return jnp.clip(drawn, min=-bound, max=bound).astype(held_as)


def setup_inputs(seed: int = 0) -> dict:
    keys = jax.random.split(jax.random.key(seed), 6)
    return {
        "queries": draw_queries(jax.random.fold_in(keys[5], 71), 0),
        "key_states": draw_key_states(jax.random.fold_in(keys[5], 71), 0),
        "value_states": normal_values(keys[2], (TOKENS, HEADS * HEAD), 1.0, 6.0, ((0, 128), (1, 2))),
        "out_grad": normal_values(keys[3], (TOKENS, HEADS * HEAD), 1.0, 6.0, ((0, 128), (1, 2))),
        "tile_mask": draw_tile_mask(jax.random.fold_in(keys[5], 71), 0),
    }


def expand_mask(mask_rows, tile_rows):
    grown = jnp.repeat(jnp.repeat(mask_rows, tile_rows, axis=0), tile_rows, axis=1)
    return grown > 0

def device_block(inputs):
    queries, grads_in, key_band, value_band, mask_rows = inputs
    row_count = queries.shape[0]
    score_scale = 1.0 / math.sqrt(HEAD)
    query_heads = queries.reshape(row_count, HEADS, HEAD).astype(jnp.float32)
    grad_heads = grads_in.reshape(row_count, HEADS, HEAD).astype(jnp.float32)
    key_heads = key_band.reshape(3 * row_count, HEADS, HEAD).astype(jnp.float32)
    value_heads = value_band.reshape(3 * row_count, HEADS, HEAD).astype(jnp.float32)
    live_mask = expand_mask(mask_rows, TILE)[None]
    scores = jnp.einsum('qhd,khd->hqk', query_heads, key_heads) * score_scale
    scores = jnp.where(live_mask, scores, -jnp.inf)
    row_top = lax.optimization_barrier(jnp.max(scores, axis=-1, keepdims=True))
    log_total = row_top + jnp.log(lax.optimization_barrier(jnp.sum(jnp.exp(scores - row_top), axis=-1, keepdims=True)))
    attn_weights = jnp.exp(scores - log_total)
    dweights = jnp.einsum('qhd,khd->hqk', grad_heads, value_heads)
    row_delta = lax.optimization_barrier(jnp.sum(attn_weights * dweights, axis=-1, keepdims=True))
    dscores = (attn_weights * (dweights - row_delta) * score_scale).astype(jnp.bfloat16)
    weights_low = attn_weights.astype(jnp.bfloat16)
    dscores_wide = lax.optimization_barrier(dscores).astype(jnp.float32)
    weights_wide = lax.optimization_barrier(weights_low).astype(jnp.float32)
    grad_query = jnp.einsum('hqk,khd->qhd', dscores_wide, key_heads).reshape(row_count, HEADS * HEAD)
    key_part = jnp.einsum('hqk,qhd->khd', dscores_wide, query_heads).reshape(3 * row_count, HEADS * HEAD)
    value_part = jnp.einsum('hqk,qhd->khd', weights_wide, grad_heads).reshape(3 * row_count, HEADS * HEAD)
    return (grad_query.astype(jnp.bfloat16), key_part.astype(jnp.bfloat16), value_part.astype(jnp.bfloat16))

def reference(queries, key_states, value_states, out_grad, tile_mask):
    row_count = TILE * TPD
    query_groups = queries.reshape(N_CTX, row_count, HEADS * HEAD)
    grad_groups = out_grad.reshape(N_CTX, row_count, HEADS * HEAD)
    key_groups = key_states.reshape(N_CTX, row_count, HEADS * HEAD)
    value_groups = value_states.reshape(N_CTX, row_count, HEADS * HEAD)
    key_bands = jnp.concatenate([jnp.roll(key_groups, 1, 0), key_groups, jnp.roll(key_groups, -1, 0)], axis=1)
    value_bands = jnp.concatenate([jnp.roll(value_groups, 1, 0), value_groups, jnp.roll(value_groups, -1, 0)], axis=1)
    mask_groups = tile_mask.reshape(N_CTX, TPD, 3 * TPD)
    grad_query, key_part, value_part = lax.map(device_block, (query_groups, grad_groups, key_bands, value_bands, mask_groups))

    def combine(partials):
        wide = partials.astype(jnp.float32)
        own_part = wide[:, row_count:2 * row_count]
        from_next = jnp.roll(wide[:, :row_count], -1, 0)
        from_prev = jnp.roll(wide[:, 2 * row_count:], 1, 0)
        return (own_part + from_next + from_prev).astype(jnp.bfloat16).reshape(TOKENS, HEADS * HEAD)
    return (grad_query.reshape(TOKENS, HEADS * HEAD), combine(key_part), combine(value_part))
```

```python
import functools
import math

import jax
import jax.numpy as jnp
from jax import lax
from jax.experimental import pallas as pl
from jax.experimental.pallas import tpu as pltpu
from jax.sharding import PartitionSpec as P

HEAD = 128
H = 20
TILE = 128
ROWS = 256
CHUNKS = (5, 5, 5, 5)
SCALE = 1.0 / math.sqrt(HEAD)
LOG2E = math.log2(math.e)
DEAD = -1e30
BF16 = jnp.bfloat16
PARAMS = pltpu.CompilerParams(vmem_limit_bytes=66_000_000)

NT = (((1,), (1,)), ((), ()))
NN = (((1,), (0,)), ((), ()))
TN = (((0,), (0,)), ((), ()))


def dot(a, b, dims):
    return lax.dot_general(a, b, dims, preferred_element_type=jnp.float32)


def split_rows(side, rows, keep_ref, send_ref):
    @pl.when(side == 0)
    def _():
        keep_ref[...] = rows[:TILE]
        send_ref[...] = rows[TILE:]

    @pl.when(side == 1)
    def _():
        keep_ref[...] = rows[TILE:]
        send_ref[...] = rows[:TILE]


def attn_kernel(
    side_ref, q_ref, do_ref, k_ref, v_ref, nk_ref, nv_ref, far_ref, bias_ref, *refs
):
    keep_ref, send_ref, own_ref, near_out, far_out = refs[-5:]
    q, do = q_ref[...], do_ref[...]
    groups = [
        (nk_ref[...], nv_ref[...], near_out),
        (k_ref[...], v_ref[...], own_ref),
        (far_ref[0], far_ref[1], far_out),
    ]
    ts, tops = [], []
    for g, (kg, _, _) in enumerate(groups):
        s = dot(kg, q, NT) * (SCALE * LOG2E)
        for half in range(2):
            t = s[half * TILE : (half + 1) * TILE] + bias_ref[2 * g + half : 2 * g + half + 1, :]
            ts.append(t)
            tops.append(jnp.max(t, axis=0, keepdims=True))
    top = functools.reduce(jnp.maximum, tops)
    es = [jnp.exp2(t - top) for t in ts]
    total = sum(jnp.sum(e, axis=0, keepdims=True) for e in es)
    dps, acc = [], 0.0
    for g, (_, vg, _) in enumerate(groups):
        dp = dot(vg, do, NT)
        for half in range(2):
            d = dp[half * TILE : (half + 1) * TILE]
            dps.append(d)
            acc = acc + jnp.sum(es[2 * g + half] * d, axis=0, keepdims=True)
    inv = 1.0 / total
    delta = acc * inv
    inv_scaled = inv * SCALE
    dq = None
    for g, (kg, _, out) in enumerate(groups):
        pair = (2 * g, 2 * g + 1)
        w = jnp.concatenate([(es[j] * inv).astype(BF16) for j in pair], axis=0)
        ds = jnp.concatenate(
            [((es[j] * inv_scaled) * (dps[j] - delta)).astype(BF16) for j in pair], axis=0
        )
        out[0] = dot(ds, q, NN).astype(BF16)
        out[1] = dot(w, do, NN).astype(BF16)
        part = dot(ds, kg, TN)
        dq = part if dq is None else dq + part
    split_rows(side_ref[0], dq.astype(BF16), keep_ref, send_ref)


def attn_chunk(side, q, do, k, v, near_k, near_v, far, bias, out, h0, hc):
    block = pl.BlockSpec((ROWS, HEAD), lambda i, s: (0, h0 + i))
    pair = pl.BlockSpec((2, ROWS, HEAD), lambda i, s: (0, 0, i))
    specs = [block] * 6 + [pair, pl.BlockSpec((8, ROWS), lambda i, s: (0, 0))]
    args, alias = [q, do, k, v, near_k, near_v, far, bias], {}
    if out is not None:
        specs.append(pl.BlockSpec(memory_space=pl.ANY))
        args.append(out)
        alias = {9: 0}
    return pl.pallas_call(
        attn_kernel,
        grid_spec=pltpu.PrefetchScalarGridSpec(
            num_scalar_prefetch=1,
            grid=(hc,),
            in_specs=specs,
            out_specs=[
                pl.BlockSpec((TILE, HEAD), lambda i, s: (0, s[0] * H + h0 + i)),
                pl.BlockSpec((TILE, HEAD), lambda i, s: (0, i)),
                pair,
                pair,
                pair,
            ],
        ),
        out_shape=[
            pltpu.HBM((TILE, 2 * H * HEAD), BF16),
            pltpu.HBM((TILE, hc * HEAD), BF16),
        ]
        + [pltpu.HBM((2, ROWS, hc * HEAD), BF16)] * 3,
        input_output_aliases=alias,
        compiler_params=PARAMS,
        name="attn",
    )(side, *args)


def combine_kernel(side_ref, own_ref, fn_ref, fp_ref, *refs):
    keep_k, keep_v, send_ref = refs[-3:]
    f32 = jnp.float32
    for j, keep in enumerate((keep_k, keep_v)):
        total = own_ref[j].astype(f32) + fn_ref[j].astype(f32) + fp_ref[j].astype(f32)
        split_rows(side_ref[0], total.astype(BF16), keep, send_ref.at[pl.ds(j * TILE, TILE)])


def combine(side, own, from_near, from_far, outs, h0, hc):
    pair = pl.BlockSpec((2, ROWS, HEAD), lambda i, s: (0, 0, i))
    specs, args, alias = [pair] * 3, [own, from_near, from_far], {}
    if outs is not None:
        specs += [pl.BlockSpec(memory_space=pl.ANY)] * 2
        args += list(outs)
        alias = {4: 0, 5: 1}
    keep = pl.BlockSpec((TILE, HEAD), lambda i, s: (0, s[0] * H + h0 + i))
    return pl.pallas_call(
        combine_kernel,
        grid_spec=pltpu.PrefetchScalarGridSpec(
            num_scalar_prefetch=1,
            grid=(hc,),
            in_specs=specs,
            out_specs=[keep, keep, pl.BlockSpec((2 * TILE, HEAD), lambda i, s: (0, i))],
        ),
        out_shape=[pltpu.HBM((TILE, 2 * H * HEAD), BF16)] * 2
        + [pltpu.HBM((2 * TILE, hc * HEAD), BF16)],
        input_output_aliases=alias,
        compiler_params=PARAMS,
        name="combine",
    )(side, *args)


def place_kernel(side_ref, src_ref, *refs):
    outs = refs[len(refs) // 2 :]
    for j, out in enumerate(outs):
        out[...] = src_ref[j * TILE : (j + 1) * TILE]


def place(side, part, outs, h0, hc):
    n = len(outs)
    dest = pl.BlockSpec((TILE, HEAD), lambda i, s: (0, (1 - s[0]) * H + h0 + i))
    return pl.pallas_call(
        place_kernel,
        grid_spec=pltpu.PrefetchScalarGridSpec(
            num_scalar_prefetch=1,
            grid=(hc,),
            in_specs=[pl.BlockSpec((n * TILE, HEAD), lambda i, s: (0, i))]
            + [pl.BlockSpec(memory_space=pl.ANY)] * n,
            out_specs=[dest] * n,
        ),
        out_shape=[pltpu.HBM((TILE, 2 * H * HEAD), BF16)] * n,
        input_output_aliases={2 + j: j for j in range(n)},
        compiler_params=PARAMS,
        name="place",
    )(side, part, *outs)


def pack_kernel(k_ref, v_ref, out_ref):
    out_ref[0] = k_ref[...]
    out_ref[1] = v_ref[...]


def pack(k, v, h0, hc):
    block = pl.BlockSpec((ROWS, HEAD), lambda i: (0, h0 + i))
    return pl.pallas_call(
        pack_kernel,
        grid=(hc,),
        in_specs=[block] * 2,
        out_specs=pl.BlockSpec((2, ROWS, HEAD), lambda i: (0, 0, i)),
        out_shape=pltpu.HBM((2, ROWS, hc * HEAD), BF16),
        compiler_params=PARAMS,
        name="pack",
    )(k, v)


def near_swap(x):
    return lax.ppermute(x, "ctx", [(i, i ^ 1) for i in range(lax.axis_size("ctx"))])


def far_swap(x):
    count = lax.axis_size("ctx")
    return lax.ppermute(x, "ctx", [(i, (i + 2 * (i % 2) - 1) % count) for i in range(count)])


def swap(x):
    return lax.ppermute(x, "section", [(0, 1), (1, 0)])


def split_heads(sizes):
    return [(sum(sizes[:n]), size) for n, size in enumerate(sizes)]


def on_device(queries, key_states, value_states, out_grad, tile_mask):
    position = lax.axis_index("ctx")
    side = lax.axis_index("section").astype(jnp.int32).reshape(1)
    own_mask = lax.dynamic_slice_in_dim(tile_mask, position * 2, 2, 0)
    bias = jnp.where(jnp.repeat(own_mask.T, TILE, axis=1) > 0, 0.0, DEAD).astype(jnp.float32)
    before, own, after = bias[0:2], bias[2:4], bias[4:6]
    odd = position % 2 == 1
    near = jnp.where(odd, before, after)
    far = jnp.where(odd, after, before)
    bias = jnp.concatenate([near, own, far, jnp.zeros((2, ROWS), jnp.float32)], axis=0)

    spans = split_heads(CHUNKS)
    count = len(spans)
    near_k, near_v = near_swap(key_states), near_swap(value_states)
    packs, source = [pack(key_states, value_states, *spans[0])], key_states
    source, near_k = lax.optimization_barrier((source, near_k))
    for h0, hc in spans[1:]:
        packs.append(pack(source, value_states, h0, hc))
        source, packs[-1] = lax.optimization_barrier((source, packs[-1]))
    fars = [far_swap(packs[0]), far_swap(packs[1])]
    bias, *_ = lax.optimization_barrier((bias, *packs))

    out_q, out_kv = None, None
    q_parts, kv_parts, owns, from_far, from_near = [], [], [], [], []

    def finish(n, own):
        nonlocal out_kv
        h0, hc = spans[n]
        *out_kv, send = combine(side, own, from_near[n], from_far[n], out_kv, h0, hc)
        kv_parts.append(swap(send))

    def after(arrived, *values):
        held = lax.optimization_barrier((*values, *(where[i] for where, i in arrived)))
        for (where, i), value in zip(arrived, held[len(values) :]):
            where[i] = value
        return held[: len(values)]

    nears = []
    for n, (h0, hc) in enumerate(spans):
        if n >= 1:
            arrived = [(fars, n)] + ([(from_far, n - 2)] if n >= 2 else [])
            (near_part,) = after(arrived, nears[n - 1])
            from_near.append(near_swap(near_part))
            if n >= 2:
                finish(n - 2, owns[n - 2])
        out_q, send_q, own, near_part, far_part = attn_chunk(
            side, queries, out_grad, key_states, value_states, near_k, near_v, fars[n], bias,
            out_q, h0, hc,
        )
        arrived = []
        if n >= 1:
            arrived += [(q_parts, n - 1), (from_near, n - 1)]
        if 2 <= n < count - 1:
            arrived.append((kv_parts, n - 2))
        if n + 2 < count:
            arrived.append((packs, n + 2))
        send_q, own, near_part, far_part = after(arrived, send_q, own, near_part, far_part)
        from_far.append(far_swap(far_part))
        if n + 2 < count:
            fars.append(far_swap(packs[n + 2]))
        q_parts.append(swap(send_q))
        nears.append(near_part)
        owns.append(own)
    from_near.append(near_swap(nears[-1]))
    for n in range(max(count - 2, 0), count):
        finish(n, owns[n])
    for (h0, hc), part in zip(spans, q_parts):
        (out_q,) = place(side, part, [out_q], h0, hc)
    for (h0, hc), part in zip(spans, kv_parts):
        out_kv = place(side, part, out_kv, h0, hc)
    return (out_q, *out_kv)


def solution(mesh):
    placed = P("ctx", "section")
    out = P(("ctx", "section"), None)
    return jax.shard_map(
        on_device,
        mesh=mesh,
        in_specs=(placed, placed, placed, placed, P()),
        out_specs=(out, out, out),
        check_vma=False,
    )
```

```python
import functools
import math

import jax
import jax.numpy as jnp
from jax import lax
from jax.experimental import pallas as pl
from jax.experimental.pallas import tpu as pltpu
from jax.sharding import PartitionSpec as P

HEAD = 128
H = 20
TILE = 128
ROWS = 256
CHUNKS = (7, 7, 6)
SCALE = 1.0 / math.sqrt(HEAD)
LOG2E = math.log2(math.e)
DEAD = -1e30
BF16 = jnp.bfloat16
PARAMS = pltpu.CompilerParams(vmem_limit_bytes=66_000_000)

NT = (((1,), (1,)), ((), ()))
NN = (((1,), (0,)), ((), ()))
TN = (((0,), (0,)), ((), ()))


def dot(a, b, dims):
    return lax.dot_general(a, b, dims, preferred_element_type=jnp.float32)


def split_rows(side, rows, keep_ref, send_ref):
    @pl.when(side == 0)
    def _():
        keep_ref[...] = rows[:TILE]
        send_ref[...] = rows[TILE:]

    @pl.when(side == 1)
    def _():
        keep_ref[...] = rows[TILE:]
        send_ref[...] = rows[:TILE]


def attn_kernel(
    side_ref, q_ref, do_ref, k_ref, v_ref, nk_ref, nv_ref, far_ref, bias_ref, *refs
):
    keep_ref, send_ref, own_ref, near_out, far_out = refs[-5:]
    q, do = q_ref[...], do_ref[...]
    groups = [
        (nk_ref[...], nv_ref[...], near_out),
        (k_ref[...], v_ref[...], own_ref),
        (far_ref[0], far_ref[1], far_out),
    ]
    ts, tops = [], []
    for g, (kg, _, _) in enumerate(groups):
        s = dot(kg, q, NT) * (SCALE * LOG2E)
        for half in range(2):
            t = s[half * TILE : (half + 1) * TILE] + bias_ref[2 * g + half : 2 * g + half + 1, :]
            ts.append(t)
            tops.append(jnp.max(t, axis=0, keepdims=True))
    top = functools.reduce(jnp.maximum, tops)
    es = [jnp.exp2(t - top) for t in ts]
    total = sum(jnp.sum(e, axis=0, keepdims=True) for e in es)
    dps, acc = [], 0.0
    for g, (_, vg, _) in enumerate(groups):
        dp = dot(vg, do, NT)
        for half in range(2):
            d = dp[half * TILE : (half + 1) * TILE]
            dps.append(d)
            acc = acc + jnp.sum(es[2 * g + half] * d, axis=0, keepdims=True)
    inv = 1.0 / total
    delta = acc * inv
    inv_scaled = inv * SCALE
    dq = None
    for g, (kg, _, out) in enumerate(groups):
        pair = (2 * g, 2 * g + 1)
        w = jnp.concatenate([(es[j] * inv).astype(BF16) for j in pair], axis=0)
        ds = jnp.concatenate(
            [((es[j] * inv_scaled) * (dps[j] - delta)).astype(BF16) for j in pair], axis=0
        )
        out[0] = dot(ds, q, NN).astype(BF16)
        out[1] = dot(w, do, NN).astype(BF16)
        part = dot(ds, kg, TN)
        dq = part if dq is None else dq + part
    split_rows(side_ref[0], dq.astype(BF16), keep_ref, send_ref)


def attn_chunk(side, q, do, k, v, near_k, near_v, far, bias, out, h0, hc):
    block = pl.BlockSpec((ROWS, HEAD), lambda i, s: (0, h0 + i))
    pair = pl.BlockSpec((2, ROWS, HEAD), lambda i, s: (0, 0, i))
    specs = [block] * 6 + [pair, pl.BlockSpec((8, ROWS), lambda i, s: (0, 0))]
    args, alias = [q, do, k, v, near_k, near_v, far, bias], {}
    if out is not None:
        specs.append(pl.BlockSpec(memory_space=pl.ANY))
        args.append(out)
        alias = {9: 0}
    return pl.pallas_call(
        attn_kernel,
        grid_spec=pltpu.PrefetchScalarGridSpec(
            num_scalar_prefetch=1,
            grid=(hc,),
            in_specs=specs,
            out_specs=[
                pl.BlockSpec((TILE, HEAD), lambda i, s: (0, s[0] * H + h0 + i)),
                pl.BlockSpec((TILE, HEAD), lambda i, s: (0, i)),
                pair,
                pair,
                pair,
            ],
        ),
        out_shape=[
            pltpu.HBM((TILE, 2 * H * HEAD), BF16),
            pltpu.HBM((TILE, hc * HEAD), BF16),
        ]
        + [pltpu.HBM((2, ROWS, hc * HEAD), BF16)] * 3,
        input_output_aliases=alias,
        compiler_params=PARAMS,
        name="attn",
    )(side, *args)


def columns(side, h0, hc):
    return pl.ds(pl.multiple_of(side * (H * HEAD) + h0 * HEAD, HEAD), hc * HEAD)


def run_all(copies):
    for copy in copies:
        copy.start()
    for copy in copies:
        copy.wait()


def combine_kernel(h0, hc, side_ref, own_ref, near_ref, far_ref, *refs):
    keep_k, keep_v, send_ref, parts, kept, sent, in_sems, out_sems = refs[-8:]
    f32, side = jnp.float32, side_ref[0]
    fetches = [
        [
            pltpu.make_async_copy(src.at[j], parts.at[j, n], in_sems.at[j, n])
            for n, src in enumerate((own_ref, near_ref, far_ref))
        ]
        for j in range(2)
    ]
    for copy in fetches[0] + fetches[1]:
        copy.start()
    leaving = []
    for j, keep in enumerate((keep_k, keep_v)):
        for copy in fetches[j]:
            copy.wait()
        total = parts[j, 0].astype(f32) + parts[j, 1].astype(f32) + parts[j, 2].astype(f32)
        split_rows(side, total.astype(BF16), kept.at[j], sent.at[j])
        leaving += [
            pltpu.make_async_copy(
                sent.at[j], send_ref.at[pl.ds(j * TILE, TILE)], out_sems.at[j, 0]
            ),
            pltpu.make_async_copy(
                kept.at[j], keep.at[:, columns(side, h0, hc)], out_sems.at[j, 1]
            ),
        ]
        for copy in leaving[-2:]:
            copy.start()
    for copy in leaving:
        copy.wait()


def combine(side, own, from_near, from_far, outs, h0, hc):
    width = hc * HEAD
    anywhere = pl.BlockSpec(memory_space=pl.ANY)
    args, alias = [own, from_near, from_far], {}
    if outs is not None:
        args += list(outs)
        alias = {4: 0, 5: 1}
    return pl.pallas_call(
        functools.partial(combine_kernel, h0, hc),
        grid_spec=pltpu.PrefetchScalarGridSpec(
            num_scalar_prefetch=1,
            grid=(1,),
            in_specs=[anywhere] * len(args),
            out_specs=[anywhere] * 3,
            scratch_shapes=[
                pltpu.VMEM((2, 3, ROWS, width), BF16),
                pltpu.VMEM((2, TILE, width), BF16),
                pltpu.VMEM((2, TILE, width), BF16),
                pltpu.SemaphoreType.DMA((2, 3)),
                pltpu.SemaphoreType.DMA((2, 2)),
            ],
        ),
        out_shape=[pltpu.HBM((TILE, 2 * H * HEAD), BF16)] * 2
        + [pltpu.HBM((2 * TILE, width), BF16)],
        input_output_aliases=alias,
        compiler_params=PARAMS,
        name="combine",
    )(side, *args)


def place_kernel(moves, side_ref, *refs):
    sems = refs[-1]
    outs = refs[len(refs) - 1 - max(o for _, _, o, _, _ in moves) - 1 : -1]
    copies = [
        pltpu.make_async_copy(
            refs[part].at[pl.ds(row, TILE)],
            outs[o].at[:, columns(1 - side_ref[0], h0, hc)],
            sems.at[n],
        )
        for n, (part, row, o, h0, hc) in enumerate(moves)
    ]
    run_all(copies)


def place(side, parts, outs, spans):
    moves = [
        (p, o * TILE, o, h0, hc) for p, (h0, hc) in enumerate(spans) for o in range(len(outs))
    ]
    return pl.pallas_call(
        functools.partial(place_kernel, moves),
        grid_spec=pltpu.PrefetchScalarGridSpec(
            num_scalar_prefetch=1,
            grid=(1,),
            in_specs=[pl.BlockSpec(part.shape, lambda i, s: (0, 0)) for part in parts]
            + [pl.BlockSpec(memory_space=pl.ANY)] * len(outs),
            out_specs=[pl.BlockSpec(memory_space=pl.ANY)] * len(outs),
            scratch_shapes=[pltpu.SemaphoreType.DMA((len(moves),))],
        ),
        out_shape=[pltpu.HBM((TILE, 2 * H * HEAD), BF16)] * len(outs),
        input_output_aliases={1 + len(parts) + j: j for j in range(len(outs))},
        compiler_params=PARAMS,
        name="place",
    )(side, *parts, *outs)


def pack_kernel(spans, k_ref, v_ref, *refs):
    count = len(spans)
    outs, stages, sems = refs[:count], refs[count : 2 * count], refs[-1]
    moves = []
    for n, (h0, hc) in enumerate(spans):
        for j, src in enumerate((k_ref, v_ref)):
            cols = pl.ds(h0 * HEAD, hc * HEAD)
            moves.append(
                (
                    pltpu.make_async_copy(src.at[:, cols], stages[n].at[j], sems.at[n, j, 0]),
                    pltpu.make_async_copy(stages[n].at[j], outs[n].at[j], sems.at[n, j, 1]),
                )
            )
    for fetch, _ in moves:
        fetch.start()
    for fetch, store in moves:
        fetch.wait()
        store.start()
    for _, store in moves:
        store.wait()


def pack(k, v, spans):
    return pl.pallas_call(
        functools.partial(pack_kernel, spans),
        grid=(1,),
        in_specs=[pl.BlockSpec(memory_space=pl.ANY)] * 2,
        out_specs=[pl.BlockSpec(memory_space=pl.ANY)] * len(spans),
        out_shape=[pltpu.HBM((2, ROWS, hc * HEAD), BF16) for _, hc in spans],
        scratch_shapes=[pltpu.VMEM((2, ROWS, hc * HEAD), BF16) for _, hc in spans]
        + [pltpu.SemaphoreType.DMA((len(spans), 2, 2))],
        compiler_params=PARAMS,
        name="pack",
    )(k, v)


def near_swap(x):
    return lax.ppermute(x, "ctx", [(i, i ^ 1) for i in range(lax.axis_size("ctx"))])


def far_swap(x):
    count = lax.axis_size("ctx")
    return lax.ppermute(x, "ctx", [(i, (i + 2 * (i % 2) - 1) % count) for i in range(count)])


def swap(x):
    return lax.ppermute(x, "section", [(0, 1), (1, 0)])


def split_heads(sizes):
    return [(sum(sizes[:n]), size) for n, size in enumerate(sizes)]


def on_device(queries, key_states, value_states, out_grad, tile_mask):
    position = lax.axis_index("ctx")
    side = lax.axis_index("section").astype(jnp.int32).reshape(1)
    own_mask = lax.dynamic_slice_in_dim(tile_mask, position * 2, 2, 0)
    bias = jnp.where(jnp.repeat(own_mask.T, TILE, axis=1) > 0, 0.0, DEAD).astype(jnp.float32)
    before, own, after = bias[0:2], bias[2:4], bias[4:6]
    odd = position % 2 == 1
    near = jnp.where(odd, before, after)
    far = jnp.where(odd, after, before)
    bias = jnp.concatenate([near, own, far, jnp.zeros((2, ROWS), jnp.float32)], axis=0)

    spans = split_heads(CHUNKS)
    count = len(spans)
    near_k, near_v = near_swap(key_states), near_swap(value_states)
    packs = list(pack(key_states, value_states, spans[:1]))
    later_keys, near_k = lax.optimization_barrier((key_states, near_k))
    packs += pack(later_keys, value_states, spans[1:])
    fars = [far_swap(packs[0]), far_swap(packs[1])]
    bias, *_ = lax.optimization_barrier((bias, *packs))

    out_q, out_kv = None, None
    q_parts, kv_parts, owns, from_far, from_near = [], [], [], [], []

    def finish(n, own):
        nonlocal out_kv
        h0, hc = spans[n]
        *out_kv, send = combine(side, own, from_near[n], from_far[n], out_kv, h0, hc)
        kv_parts.append(swap(send))

    def after(arrived, *values):
        held = lax.optimization_barrier((*values, *(where[i] for where, i in arrived)))
        for (where, i), value in zip(arrived, held[len(values) :]):
            where[i] = value
        return held[: len(values)]

    nears = []
    for n, (h0, hc) in enumerate(spans):
        if n >= 1:
            arrived = [(fars, n)] + ([(from_far, n - 2)] if n >= 2 else [])
            (near_part,) = after(arrived, nears[n - 1])
            from_near.append(near_swap(near_part))
            if n >= 2:
                finish(n - 2, owns[n - 2])
        out_q, send_q, own, near_part, far_part = attn_chunk(
            side, queries, out_grad, key_states, value_states, near_k, near_v, fars[n], bias,
            out_q, h0, hc,
        )
        arrived = []
        if n >= 1:
            arrived += [(q_parts, n - 1), (from_near, n - 1)]
        if 2 <= n < count - 1:
            arrived.append((kv_parts, n - 2))
        if n + 2 < count:
            arrived.append((packs, n + 2))
        send_q, own, near_part, far_part = after(arrived, send_q, own, near_part, far_part)
        from_far.append(far_swap(far_part))
        if n + 2 < count:
            fars.append(far_swap(packs[n + 2]))
        q_parts.append(swap(send_q))
        nears.append(near_part)
        owns.append(own)
    from_near.append(near_swap(nears[-1]))
    for n in range(max(count - 2, 0), count):
        finish(n, owns[n])
    (out_q,) = place(side, q_parts, [out_q], spans)
    out_kv = place(side, kv_parts[:-1], out_kv, spans[:-1])
    out_kv = place(side, kv_parts[-1:], out_kv, spans[-1:])
    return (out_q, *out_kv)


def solution(mesh):
    placed = P("ctx", "section")
    out = P(("ctx", "section"), None)
    return jax.shard_map(
        on_device,
        mesh=mesh,
        in_specs=(placed, placed, placed, placed, P()),
        out_specs=(out, out, out),
        check_vma=False,
    )
```

```python
import functools
import math

import jax
import jax.numpy as jnp
from jax import lax
from jax.experimental import pallas as pl
from jax.experimental.pallas import tpu as pltpu
from jax.sharding import PartitionSpec as P

HEAD = 128
H = 20
TILE = 128
ROWS = 256
CHUNKS = (7, 7, 6)
RELAYED = (1,)
SCALE = 1.0 / math.sqrt(HEAD)
LOG2E = math.log2(math.e)
DEAD = -1e30
BF16 = jnp.bfloat16
COST = pl.CostEstimate(flops=1000, transcendentals=0, bytes_accessed=1000)
PARAMS = pltpu.CompilerParams(vmem_limit_bytes=67_000_000)

NT = (((1,), (1,)), ((), ()))
NN = (((1,), (0,)), ((), ()))
TN = (((0,), (0,)), ((), ()))


def dot(a, b, dims):
    return lax.dot_general(a, b, dims, preferred_element_type=jnp.float32)


def split_rows(side, rows, keep_ref, send_ref):
    @pl.when(side == 0)
    def _():
        keep_ref[...] = rows[:TILE]
        send_ref[...] = rows[TILE:]

    @pl.when(side == 1)
    def _():
        keep_ref[...] = rows[TILE:]
        send_ref[...] = rows[:TILE]


def attn_kernel(
    side_ref, q_ref, do_ref, k_ref, v_ref, nk_ref, nv_ref, far_ref, bias_ref, *refs
):
    keep_ref, send_ref, own_ref, near_out, far_out = refs[-5:]
    q, do = q_ref[...], do_ref[...]
    groups = [
        (nk_ref[...], nv_ref[...], near_out),
        (k_ref[...], v_ref[...], own_ref),
        (far_ref[0], far_ref[1], far_out),
    ]
    ts, tops = [], []
    for g, (kg, _, _) in enumerate(groups):
        s = dot(kg, q, NT) * (SCALE * LOG2E)
        for half in range(2):
            t = s[half * TILE : (half + 1) * TILE] + bias_ref[2 * g + half : 2 * g + half + 1, :]
            ts.append(t)
            tops.append(jnp.max(t, axis=0, keepdims=True))
    top = functools.reduce(jnp.maximum, tops)
    es = [jnp.exp2(t - top) for t in ts]
    total = sum(jnp.sum(e, axis=0, keepdims=True) for e in es)
    dps, acc = [], 0.0
    for g, (_, vg, _) in enumerate(groups):
        dp = dot(vg, do, NT)
        for half in range(2):
            d = dp[half * TILE : (half + 1) * TILE]
            dps.append(d)
            acc = acc + jnp.sum(es[2 * g + half] * d, axis=0, keepdims=True)
    inv = 1.0 / total
    delta = acc * inv
    inv_scaled = inv * SCALE
    dq = None
    for g, (kg, _, out) in enumerate(groups):
        pair = (2 * g, 2 * g + 1)
        w = jnp.concatenate([(es[j] * inv).astype(BF16) for j in pair], axis=0)
        ds = jnp.concatenate(
            [((es[j] * inv_scaled) * (dps[j] - delta)).astype(BF16) for j in pair], axis=0
        )
        out[0] = dot(ds, q, NN).astype(BF16)
        out[1] = dot(w, do, NN).astype(BF16)
        part = dot(ds, kg, TN)
        dq = part if dq is None else dq + part
    split_rows(side_ref[0], dq.astype(BF16), keep_ref, send_ref)


def attn_chunk(side, q, do, k, v, near_k, near_v, far, bias, out, h0, hc):
    block = pl.BlockSpec((ROWS, HEAD), lambda i, s: (0, h0 + i))
    pair = pl.BlockSpec((2, ROWS, HEAD), lambda i, s: (0, 0, i))
    specs = [block] * 6 + [pair, pl.BlockSpec((8, ROWS), lambda i, s: (0, 0))]
    args, alias = [q, do, k, v, near_k, near_v, far, bias], {}
    if out is not None:
        specs.append(pl.BlockSpec(memory_space=pl.ANY))
        args.append(out)
        alias = {9: 0}
    return pl.pallas_call(
        attn_kernel,
        grid_spec=pltpu.PrefetchScalarGridSpec(
            num_scalar_prefetch=1,
            grid=(hc,),
            in_specs=specs,
            out_specs=[
                pl.BlockSpec((TILE, HEAD), lambda i, s: (0, s[0] * H + h0 + i)),
                pl.BlockSpec((TILE, HEAD), lambda i, s: (0, i)),
                pair,
                pair,
                pair,
            ],
        ),
        out_shape=[
            pltpu.HBM((TILE, 2 * H * HEAD), BF16),
            pltpu.HBM((TILE, hc * HEAD), BF16),
        ]
        + [pltpu.HBM((2, ROWS, hc * HEAD), BF16)] * 3,
        input_output_aliases=alias,
        compiler_params=PARAMS,
        cost_estimate=COST,
        name="attn",
    )(side, *args)


def columns(side, h0, hc):
    return pl.ds(pl.multiple_of(side * (H * HEAD) + h0 * HEAD, HEAD), hc * HEAD)


def run_all(copies):
    for copy in copies:
        copy.start()
    for copy in copies:
        copy.wait()


def combine_kernel(h0, hc, relayed, extra, moves, n_in, side_ref, *refs):
    f32, side = jnp.float32, side_ref[0]
    ins, outs = refs[:n_in], refs[n_in : n_in + 4]
    parts, kept, sent, in_sems, out_sems, carry_sems, *stages = refs[n_in + 4 :]
    keep_k, keep_v, send_ref, out_q = outs
    fetches = [
        [
            pltpu.make_async_copy(ins[n].at[j], parts.at[j, n], in_sems.at[j, n])
            for n in range(3 + relayed)
        ]
        for j in range(2)
    ]
    carries, at = [], 3 + relayed
    if extra:
        carries.append((ins[at], send_ref.at[pl.ds(2 * TILE, TILE), pl.ds(0, extra * HEAD)]))
        at += 1
    for part, row, out, o0, oc in moves:
        source = ins[at + part].at[pl.ds(row, TILE), pl.ds(0, oc * HEAD)]
        carries.append((source, (out_q, keep_k, keep_v)[out].at[:, columns(1 - side, o0, oc)]))
    carries = [
        (
            pltpu.make_async_copy(source, stages[n], carry_sems.at[n, 0]),
            pltpu.make_async_copy(stages[n], target, carry_sems.at[n, 1]),
        )
        for n, (source, target) in enumerate(carries)
    ]
    for copy in fetches[0] + fetches[1] + [fetch for fetch, _ in carries]:
        copy.start()
    leaving = []
    for j, keep in enumerate((keep_k, keep_v)):
        for copy in fetches[j]:
            copy.wait()
        far = parts[j, 2]
        if relayed:
            far = jnp.where(side_ref[1] == 1, parts[j, 3], far)
        total = parts[j, 0].astype(f32) + parts[j, 1].astype(f32) + far.astype(f32)
        split_rows(side, total.astype(BF16), kept.at[j], sent.at[j])
        leaving += [
            pltpu.make_async_copy(
                sent.at[j],
                send_ref.at[pl.ds(j * TILE, TILE), pl.ds(0, hc * HEAD)],
                out_sems.at[j, 0],
            ),
            pltpu.make_async_copy(
                kept.at[j], keep.at[:, columns(side, h0, hc)], out_sems.at[j, 1]
            ),
        ]
        for copy in leaving[-2:]:
            copy.start()
    for fetch, store in carries:
        fetch.wait()
        store.start()
        leaving.append(store)
    for copy in leaving:
        copy.wait()


def combine(side, own, from_near, from_far, out_q, out_kv, send_q, extra, arrived, moves, h0, hc):
    width, relayed = hc * HEAD, len(from_far) - 1
    anywhere = pl.BlockSpec(memory_space=pl.ANY)
    args = [own, from_near, *from_far, *([send_q] if extra else []), *arrived]
    alias = {1 + len(args): 3}
    args.append(out_q)
    if out_kv is not None:
        alias |= {1 + len(args): 0, 2 + len(args): 1}
        args += list(out_kv)
    send_shape = (3 * TILE, max(hc, extra) * HEAD) if extra else (2 * TILE, width)
    stages = ([(TILE, extra * HEAD)] if extra else []) + [(TILE, m[4] * HEAD) for m in moves]
    whole = pltpu.HBM((TILE, 2 * H * HEAD), BF16)
    return pl.pallas_call(
        functools.partial(combine_kernel, h0, hc, relayed, extra, moves, len(args)),
        grid_spec=pltpu.PrefetchScalarGridSpec(
            num_scalar_prefetch=1,
            grid=(1,),
            in_specs=[anywhere] * len(args),
            out_specs=[anywhere] * 4,
            scratch_shapes=[
                pltpu.VMEM((2, 3 + relayed, ROWS, width), BF16),
                pltpu.VMEM((2, TILE, width), BF16),
                pltpu.VMEM((2, TILE, width), BF16),
                pltpu.SemaphoreType.DMA((2, 3 + relayed)),
                pltpu.SemaphoreType.DMA((2, 2)),
                pltpu.SemaphoreType.DMA((max(len(stages), 1), 2)),
            ]
            + [pltpu.VMEM(shape, BF16) for shape in stages],
        ),
        out_shape=[whole, whole, pltpu.HBM(send_shape, BF16), whole],
        input_output_aliases=alias,
        compiler_params=PARAMS,
        cost_estimate=COST,
        name="combine",
    )(side, *args)


def place_kernel(moves, side_ref, *refs):
    sems = refs[-1]
    outs = refs[-4:-1]
    run_all(
        [
            pltpu.make_async_copy(
                refs[0].at[pl.ds(row, TILE), pl.ds(0, oc * HEAD)],
                outs[out].at[:, columns(1 - side_ref[0], o0, oc)],
                sems.at[n],
            )
            for n, (row, out, o0, oc) in enumerate(moves)
        ]
    )


def place(side, part, outs, moves):
    anywhere = pl.BlockSpec(memory_space=pl.ANY)
    return pl.pallas_call(
        functools.partial(place_kernel, moves),
        grid_spec=pltpu.PrefetchScalarGridSpec(
            num_scalar_prefetch=1,
            grid=(1,),
            in_specs=[pl.BlockSpec(part.shape, lambda i, s: (0, 0))] + [anywhere] * 3,
            out_specs=[anywhere] * 3,
            scratch_shapes=[pltpu.SemaphoreType.DMA((len(moves),))],
        ),
        out_shape=[pltpu.HBM((TILE, 2 * H * HEAD), BF16)] * 3,
        input_output_aliases={2 + j: j for j in range(3)},
        compiler_params=PARAMS,
        cost_estimate=COST,
        name="place",
    )(side, part, *outs)


def pack_kernel(spans, k_ref, v_ref, *refs):
    count = len(spans)
    outs, stages, sems = refs[:count], refs[count : 2 * count], refs[-1]
    moves = []
    for n, (h0, hc) in enumerate(spans):
        for j, src in enumerate((k_ref, v_ref)):
            cols = pl.ds(h0 * HEAD, hc * HEAD)
            moves.append(
                (
                    pltpu.make_async_copy(src.at[:, cols], stages[n].at[j], sems.at[n, j, 0]),
                    pltpu.make_async_copy(stages[n].at[j], outs[n].at[j], sems.at[n, j, 1]),
                )
            )
    for fetch, _ in moves:
        fetch.start()
    for fetch, store in moves:
        fetch.wait()
        store.start()
    for _, store in moves:
        store.wait()


def pack(k, v, spans):
    return pl.pallas_call(
        functools.partial(pack_kernel, spans),
        grid=(1,),
        in_specs=[pl.BlockSpec(memory_space=pl.ANY)] * 2,
        out_specs=[pl.BlockSpec(memory_space=pl.ANY)] * len(spans),
        out_shape=[pltpu.HBM((2, ROWS, hc * HEAD), BF16) for _, hc in spans],
        scratch_shapes=[pltpu.VMEM((2, ROWS, hc * HEAD), BF16) for _, hc in spans]
        + [pltpu.SemaphoreType.DMA((len(spans), 2, 2))],
        compiler_params=PARAMS,
        cost_estimate=COST,
        name="pack",
    )(k, v)


def near_swap(x):
    return lax.ppermute(x, "ctx", [(i, i ^ 1) for i in range(lax.axis_size("ctx"))])


def corners():
    count = lax.axis_size("ctx")
    return (0, count // 2 - 1, count // 2, count - 1)


def far_pairs():
    count = lax.axis_size("ctx")
    return [(i, (i + 2 * (i % 2) - 1) % count) for i in range(count)]


def far_swap(x, in_legs=False):
    half = lax.axis_size("ctx") // 2
    pairs = [(i, j ^ half if in_legs and i in corners() else j) for i, j in far_pairs()]
    return lax.ppermute(x, "ctx", pairs)


def across_x(x):
    half = lax.axis_size("ctx") // 2
    return lax.ppermute(x, "ctx", [(i, i ^ half) for i in corners()])


def swap(x):
    return lax.ppermute(x, "section", [(0, 1), (1, 0)])


def split_heads(sizes):
    return [(sum(sizes[:n]), size) for n, size in enumerate(sizes)]


def on_device(queries, key_states, value_states, out_grad, tile_mask):
    position = lax.axis_index("ctx")
    at_corner = functools.reduce(jnp.logical_or, [position == i for i in corners()])
    side = jnp.stack([lax.axis_index("section").astype(jnp.int32), at_corner.astype(jnp.int32)])
    own_mask = lax.dynamic_slice_in_dim(tile_mask, position * 2, 2, 0)
    bias = jnp.where(jnp.repeat(own_mask.T, TILE, axis=1) > 0, 0.0, DEAD).astype(jnp.float32)
    before, own, after = bias[0:2], bias[2:4], bias[4:6]
    odd = position % 2 == 1
    near = jnp.where(odd, before, after)
    far = jnp.where(odd, after, before)
    bias = jnp.concatenate([near, own, far, jnp.zeros((2, ROWS), jnp.float32)], axis=0)

    spans = split_heads(CHUNKS)
    count = len(spans)
    near_k, near_v = near_swap(key_states), near_swap(value_states)
    packs = list(pack(key_states, value_states, spans[:1]))
    later_keys, near_k = lax.optimization_barrier((key_states, near_k))
    packs += pack(later_keys, value_states, spans[1:])
    fars = [far_swap(packs[0]), far_swap(packs[1])]
    bias, *_ = lax.optimization_barrier((bias, *packs))

    out_q, out_kv = None, None
    sends, kv_parts, owns, from_far, from_near = [], [], [], [], []
    first_q = None

    def arrivals(n):
        moves = [(0, 1, *spans[n]), (TILE, 2, *spans[n])]
        return moves + ([(2 * TILE, 0, *spans[n + 1])] if n + 1 < count else [])

    def finish(n):
        nonlocal out_q, out_kv
        legs = [from_far[n]]
        if n in RELAYED:
            legs.append(across_x(from_far[n]))
        last = n + 1 == count
        arrived, moves = [], []
        if n == 1:
            arrived, moves = [first_q], [(0, 0, 0, *spans[0])]
        if n >= 2:
            arrived, moves = [kv_parts[n - 2]], [(0, *move) for move in arrivals(n - 2)]
        *out_kv, send, out_q = combine(
            side, owns[n], from_near[n], legs, out_q, out_kv,
            None if last else sends[n + 1], 0 if last else spans[n + 1][1], arrived, moves, *spans[n],
        )
        kv_parts.append(swap(send))

    def after(arrived, *values):
        held = lax.optimization_barrier((*values, *(where[i] for where, i in arrived)))
        for (where, i), value in zip(arrived, held[len(values) :]):
            where[i] = value
        return held[: len(values)]

    nears = []
    for n, (h0, hc) in enumerate(spans):
        if n >= 1:
            arrived = [(fars, n)] + ([(from_far, n - 2)] if n >= 2 else [])
            (near_part,) = after(arrived, nears[n - 1])
            from_near.append(near_swap(near_part))
            if n >= 2:
                finish(n - 2)
                fars[n], out_kv[0] = lax.optimization_barrier((fars[n], out_kv[0]))
        out_q, send_q, own, near_part, far_part = attn_chunk(
            side, queries, out_grad, key_states, value_states, near_k, near_v, fars[n], bias,
            out_q, h0, hc,
        )
        arrived = [(from_near, n - 1)] if n >= 1 else []
        if n >= 2:
            arrived.append((kv_parts, n - 2))
        if n + 2 < count:
            arrived.append((packs, n + 2))
        values = (send_q, own, near_part, far_part)
        if n == 1:
            *values, first_q = after(arrived, *values, first_q)
        else:
            values = after(arrived, *values)
        send_q, own, near_part, far_part = values
        from_far.append(far_swap(far_part, n in RELAYED))
        if n + 2 < count:
            fars.append(far_swap(packs[n + 2]))
        if n == 0:
            first_q = swap(send_q)
        sends.append(send_q)
        nears.append(near_part)
        owns.append(own)
    from_near.append(near_swap(nears[-1]))
    for n in range(max(count - 2, 0), count):
        finish(n)
    for n in range(max(count - 2, 0), count):
        out_q, *out_kv = place(side, kv_parts[n], (out_q, *out_kv), arrivals(n))
    return (out_q, *out_kv)


def solution(mesh):
    placed = P("ctx", "section")
    out = P(("ctx", "section"), None)
    return jax.shard_map(
        on_device,
        mesh=mesh,
        in_specs=(placed, placed, placed, placed, P()),
        out_specs=(out, out, out),
        check_vma=False,
    )
```

```python
import functools
import math

import jax
import jax.numpy as jnp
from jax import lax
from jax.experimental import pallas as pl
from jax.experimental.pallas import tpu as pltpu
from jax.sharding import PartitionSpec as P

HEAD = 128
H = 20
TILE = 128
ROWS = 256
CHUNKS = (6, 7, 7)
RELAYED = (1,)
SCALE = 1.0 / math.sqrt(HEAD)
LOG2E = math.log2(math.e)
DEAD = -1e30
BF16 = jnp.bfloat16
COST = pl.CostEstimate(flops=1000, transcendentals=0, bytes_accessed=1000)
PARAMS = pltpu.CompilerParams(vmem_limit_bytes=67_000_000)

NT = (((1,), (1,)), ((), ()))
NN = (((1,), (0,)), ((), ()))
TN = (((0,), (0,)), ((), ()))


def dot(a, b, dims):
    return lax.dot_general(a, b, dims, preferred_element_type=jnp.float32)


def split_rows(side, rows, keep_ref, send_ref):
    @pl.when(side == 0)
    def _():
        keep_ref[...] = rows[:TILE]
        send_ref[...] = rows[TILE:]

    @pl.when(side == 1)
    def _():
        keep_ref[...] = rows[TILE:]
        send_ref[...] = rows[:TILE]


def attn_kernel(
    side_ref, q_ref, do_ref, k_ref, v_ref, nk_ref, nv_ref, far_ref, bias_ref, *refs
):
    keep_ref, send_ref, own_ref, near_out, far_out = refs[-5:]
    q, do = q_ref[...], do_ref[...]
    groups = [
        (nk_ref[...], nv_ref[...], near_out),
        (k_ref[...], v_ref[...], own_ref),
        (far_ref[0], far_ref[1], far_out),
    ]
    ts, tops = [], []
    for g, (kg, _, _) in enumerate(groups):
        s = dot(kg, q, NT) * (SCALE * LOG2E)
        for half in range(2):
            t = s[half * TILE : (half + 1) * TILE] + bias_ref[2 * g + half : 2 * g + half + 1, :]
            ts.append(t)
            tops.append(jnp.max(t, axis=0, keepdims=True))
    top = functools.reduce(jnp.maximum, tops)
    es = [jnp.exp2(t - top) for t in ts]
    total = sum(jnp.sum(e, axis=0, keepdims=True) for e in es)
    dps, acc = [], 0.0
    for g, (_, vg, _) in enumerate(groups):
        dp = dot(vg, do, NT)
        for half in range(2):
            d = dp[half * TILE : (half + 1) * TILE]
            dps.append(d)
            acc = acc + jnp.sum(es[2 * g + half] * d, axis=0, keepdims=True)
    inv = 1.0 / total
    delta = acc * inv
    inv_scaled = inv * SCALE
    dq = None
    for g, (kg, _, out) in enumerate(groups):
        pair = (2 * g, 2 * g + 1)
        w = jnp.concatenate([(es[j] * inv).astype(BF16) for j in pair], axis=0)
        ds = jnp.concatenate(
            [((es[j] * inv_scaled) * (dps[j] - delta)).astype(BF16) for j in pair], axis=0
        )
        out[0] = dot(ds, q, NN).astype(BF16)
        out[1] = dot(w, do, NN).astype(BF16)
        part = dot(ds, kg, TN)
        dq = part if dq is None else dq + part
    split_rows(side_ref[0], dq.astype(BF16), keep_ref, send_ref)


def attn_chunk(side, q, do, k, v, near_k, near_v, far, bias, out, h0, hc):
    block = pl.BlockSpec((ROWS, HEAD), lambda i, s: (0, h0 + i))
    pair = pl.BlockSpec((2, ROWS, HEAD), lambda i, s: (0, 0, i))
    specs = [block] * 6 + [pair, pl.BlockSpec((8, ROWS), lambda i, s: (0, 0))]
    args, alias = [q, do, k, v, near_k, near_v, far, bias], {}
    if out is not None:
        specs.append(pl.BlockSpec(memory_space=pl.ANY))
        args.append(out)
        alias = {9: 0}
    return pl.pallas_call(
        attn_kernel,
        grid_spec=pltpu.PrefetchScalarGridSpec(
            num_scalar_prefetch=1,
            grid=(hc,),
            in_specs=specs,
            out_specs=[
                pl.BlockSpec((TILE, HEAD), lambda i, s: (0, s[0] * H + h0 + i)),
                pl.BlockSpec((TILE, HEAD), lambda i, s: (0, i)),
                pair,
                pair,
                pair,
            ],
        ),
        out_shape=[
            pltpu.HBM((TILE, 2 * H * HEAD), BF16),
            pltpu.HBM((TILE, hc * HEAD), BF16),
        ]
        + [pltpu.HBM((2, ROWS, hc * HEAD), BF16)] * 3,
        input_output_aliases=alias,
        compiler_params=PARAMS,
        cost_estimate=COST,
        name="attn",
    )(side, *args)


def columns(side, h0, hc):
    return pl.ds(pl.multiple_of(side * (H * HEAD) + h0 * HEAD, HEAD), hc * HEAD)


def run_all(copies):
    for copy in copies:
        copy.start()
    for copy in copies:
        copy.wait()


def combine_kernel(h0, hc, relayed, extra, moves, n_in, side_ref, corner_ref, *refs):
    f32, side = jnp.float32, side_ref[0]
    ins, outs = refs[:n_in], refs[n_in : n_in + 4]
    parts, kept, sent, in_sems, out_sems, carry_sems, *stages = refs[n_in + 4 :]
    keep_k, keep_v, send_ref, out_q = outs
    fetches = [
        [
            pltpu.make_async_copy(ins[n].at[j], parts.at[j, n], in_sems.at[j, n])
            for n in range(3 + relayed)
        ]
        for j in range(2)
    ]
    carries, at = [], 3 + relayed
    if extra:
        carries.append((ins[at], send_ref.at[pl.ds(2 * TILE, TILE), pl.ds(0, extra * HEAD)]))
        at += 1
    for part, row, out, o0, oc in moves:
        source = ins[at + part].at[pl.ds(row, TILE), pl.ds(0, oc * HEAD)]
        carries.append((source, (out_q, keep_k, keep_v)[out].at[:, columns(1 - side, o0, oc)]))
    carries = [
        (
            pltpu.make_async_copy(source, stages[n], carry_sems.at[n, 0]),
            pltpu.make_async_copy(stages[n], target, carry_sems.at[n, 1]),
        )
        for n, (source, target) in enumerate(carries)
    ]
    for copy in fetches[0] + fetches[1] + [fetch for fetch, _ in carries]:
        copy.start()
    leaving = []
    for j, keep in enumerate((keep_k, keep_v)):
        for copy in fetches[j]:
            copy.wait()
        far = parts[j, 2]
        if relayed:
            far = jnp.where(corner_ref[0] == 1, parts[j, 3], far)
        total = parts[j, 0].astype(f32) + parts[j, 1].astype(f32) + far.astype(f32)
        split_rows(side, total.astype(BF16), kept.at[j], sent.at[j])
        leaving += [
            pltpu.make_async_copy(
                sent.at[j],
                send_ref.at[pl.ds(j * TILE, TILE), pl.ds(0, hc * HEAD)],
                out_sems.at[j, 0],
            ),
            pltpu.make_async_copy(
                kept.at[j], keep.at[:, columns(side, h0, hc)], out_sems.at[j, 1]
            ),
        ]
        for copy in leaving[-2:]:
            copy.start()
    for fetch, store in carries:
        fetch.wait()
        store.start()
        leaving.append(store)
    for copy in leaving:
        copy.wait()


def combine(side, corner, own, from_near, from_far, out_q, out_kv, send_q, extra, arrived, moves, h0, hc):
    width, relayed = hc * HEAD, len(from_far) - 1
    anywhere = pl.BlockSpec(memory_space=pl.ANY)
    args = [own, from_near, *from_far, *([send_q] if extra else []), *arrived]
    alias = {2 + len(args): 3}
    args.append(out_q)
    if out_kv is not None:
        alias |= {2 + len(args): 0, 3 + len(args): 1}
        args += list(out_kv)
    send_shape = (3 * TILE, max(hc, extra) * HEAD) if extra else (2 * TILE, width)
    stages = ([(TILE, extra * HEAD)] if extra else []) + [(TILE, m[4] * HEAD) for m in moves]
    whole = pltpu.HBM((TILE, 2 * H * HEAD), BF16)
    return pl.pallas_call(
        functools.partial(combine_kernel, h0, hc, relayed, extra, moves, len(args)),
        grid_spec=pltpu.PrefetchScalarGridSpec(
            num_scalar_prefetch=2,
            grid=(1,),
            in_specs=[anywhere] * len(args),
            out_specs=[anywhere] * 4,
            scratch_shapes=[
                pltpu.VMEM((2, 3 + relayed, ROWS, width), BF16),
                pltpu.VMEM((2, TILE, width), BF16),
                pltpu.VMEM((2, TILE, width), BF16),
                pltpu.SemaphoreType.DMA((2, 3 + relayed)),
                pltpu.SemaphoreType.DMA((2, 2)),
                pltpu.SemaphoreType.DMA((max(len(stages), 1), 2)),
            ]
            + [pltpu.VMEM(shape, BF16) for shape in stages],
        ),
        out_shape=[whole, whole, pltpu.HBM(send_shape, BF16), whole],
        input_output_aliases=alias,
        compiler_params=PARAMS,
        cost_estimate=COST,
        name="combine",
    )(side, corner, *args)


def place_kernel(moves, side_ref, *refs):
    sems = refs[-1]
    outs = refs[-4:-1]
    run_all(
        [
            pltpu.make_async_copy(
                refs[0].at[pl.ds(row, TILE), pl.ds(0, oc * HEAD)],
                outs[out].at[:, columns(1 - side_ref[0], o0, oc)],
                sems.at[n],
            )
            for n, (row, out, o0, oc) in enumerate(moves)
        ]
    )


def place(side, part, outs, moves):
    anywhere = pl.BlockSpec(memory_space=pl.ANY)
    return pl.pallas_call(
        functools.partial(place_kernel, moves),
        grid_spec=pltpu.PrefetchScalarGridSpec(
            num_scalar_prefetch=1,
            grid=(1,),
            in_specs=[pl.BlockSpec(part.shape, lambda i, s: (0, 0))] + [anywhere] * 3,
            out_specs=[anywhere] * 3,
            scratch_shapes=[pltpu.SemaphoreType.DMA((len(moves),))],
        ),
        out_shape=[pltpu.HBM((TILE, 2 * H * HEAD), BF16)] * 3,
        input_output_aliases={2 + j: j for j in range(3)},
        compiler_params=PARAMS,
        cost_estimate=COST,
        name="place",
    )(side, part, *outs)


def pack_kernel(spans, k_ref, v_ref, *refs):
    count = len(spans)
    outs, stages, sems = refs[:count], refs[count : 2 * count], refs[-1]
    moves = []
    for n, (h0, hc) in enumerate(spans):
        for j, src in enumerate((k_ref, v_ref)):
            cols = pl.ds(h0 * HEAD, hc * HEAD)
            moves.append(
                (
                    pltpu.make_async_copy(src.at[:, cols], stages[n].at[j], sems.at[n, j, 0]),
                    pltpu.make_async_copy(stages[n].at[j], outs[n].at[j], sems.at[n, j, 1]),
                )
            )
    for fetch, _ in moves:
        fetch.start()
    for fetch, store in moves:
        fetch.wait()
        store.start()
    for _, store in moves:
        store.wait()


def pack(k, v, spans):
    return pl.pallas_call(
        functools.partial(pack_kernel, spans),
        grid=(1,),
        in_specs=[pl.BlockSpec(memory_space=pl.ANY)] * 2,
        out_specs=[pl.BlockSpec(memory_space=pl.ANY)] * len(spans),
        out_shape=[pltpu.HBM((2, ROWS, hc * HEAD), BF16) for _, hc in spans],
        scratch_shapes=[pltpu.VMEM((2, ROWS, hc * HEAD), BF16) for _, hc in spans]
        + [pltpu.SemaphoreType.DMA((len(spans), 2, 2))],
        compiler_params=PARAMS,
        cost_estimate=COST,
        name="pack",
    )(k, v)


def near_swap(x):
    return lax.ppermute(x, "ctx", [(i, i ^ 1) for i in range(lax.axis_size("ctx"))])


def corners():
    count = lax.axis_size("ctx")
    return (0, count // 2 - 1, count // 2, count - 1)


def far_pairs():
    count = lax.axis_size("ctx")
    return [(i, (i + 2 * (i % 2) - 1) % count) for i in range(count)]


def far_swap(x, in_legs=False):
    half = lax.axis_size("ctx") // 2
    pairs = [(i, j ^ half if in_legs and i in corners() else j) for i, j in far_pairs()]
    return lax.ppermute(x, "ctx", pairs)


def across_x(x):
    half = lax.axis_size("ctx") // 2
    return lax.ppermute(x, "ctx", [(i, i ^ half) for i in corners()])


def swap(x):
    return lax.ppermute(x, "section", [(0, 1), (1, 0)])


def split_heads(sizes):
    return [(sum(sizes[:n]), size) for n, size in enumerate(sizes)]


def on_device(queries, key_states, value_states, out_grad, tile_mask):
    position = lax.axis_index("ctx")
    at_corner = functools.reduce(jnp.logical_or, [position == i for i in corners()])
    at_corner = at_corner.astype(jnp.int32).reshape(1)
    side = lax.axis_index("section").astype(jnp.int32).reshape(1)
    own_mask = lax.dynamic_slice_in_dim(tile_mask, position * 2, 2, 0)
    bias = jnp.where(jnp.repeat(own_mask.T, TILE, axis=1) > 0, 0.0, DEAD).astype(jnp.float32)
    before, own, after = bias[0:2], bias[2:4], bias[4:6]
    odd = position % 2 == 1
    near = jnp.where(odd, before, after)
    far = jnp.where(odd, after, before)
    bias = jnp.concatenate([near, own, far, jnp.zeros((2, ROWS), jnp.float32)], axis=0)

    spans = split_heads(CHUNKS)
    count = len(spans)
    near_k, near_v = near_swap(key_states), near_swap(value_states)
    packs = list(pack(key_states, value_states, spans[:1]))
    later_keys, near_k = lax.optimization_barrier((key_states, near_k))
    packs += pack(later_keys, value_states, spans[1:])
    fars = [far_swap(x) for x in packs]
    bias, *_ = lax.optimization_barrier((bias, *packs))

    out_q, out_kv = None, None
    sends, kv_parts, owns, from_far, from_near = [], [], [], [], []
    first_q = None

    def arrivals(n):
        moves = [(0, 1, *spans[n]), (TILE, 2, *spans[n])]
        return moves + ([(2 * TILE, 0, *spans[n + 1])] if n + 1 < count else [])

    def finish(n):
        nonlocal out_q, out_kv
        legs = [from_far[n]]
        if n in RELAYED:
            (first_leg,) = after([(owns, n + 1)], from_far[n])
            legs.append(across_x(first_leg))
        last = n + 1 == count
        arrived, moves = [], []
        if n == 1:
            arrived, moves = [first_q], [(0, 0, 0, *spans[0])]
        if n >= 2:
            arrived, moves = [kv_parts[n - 2]], [(0, *move) for move in arrivals(n - 2)]
        *out_kv, send, out_q = combine(
            side, at_corner, owns[n], from_near[n], legs, out_q, out_kv,
            None if last else sends[n + 1], 0 if last else spans[n + 1][1], arrived, moves, *spans[n],
        )
        kv_parts.append(swap(send))

    def after(arrived, *values):
        held = lax.optimization_barrier((*values, *(where[i] for where, i in arrived)))
        for (where, i), value in zip(arrived, held[len(values) :]):
            where[i] = value
        return held[: len(values)]

    nears = []
    for n, (h0, hc) in enumerate(spans):
        if n >= 1:
            arrived = [(fars, n)] + ([(from_far, n - 2)] if n >= 2 else [])
            (near_part,) = after(arrived, nears[n - 1])
            from_near.append(near_swap(near_part))
            if n >= 2:
                finish(n - 2)
                fars[n], out_kv[0] = lax.optimization_barrier((fars[n], out_kv[0]))
        out_q, send_q, own, near_part, far_part = attn_chunk(
            side, queries, out_grad, key_states, value_states, near_k, near_v, fars[n], bias,
            out_q, h0, hc,
        )
        arrived = [(from_near, n - 1)] if n >= 1 else []
        if n >= 2:
            arrived.append((kv_parts, n - 2))
        if n >= 1 and n + 1 < count:
            arrived.append((fars, n + 1))
        values = (send_q, own, near_part, far_part)
        if n == 1:
            *values, first_q = after(arrived, *values, first_q)
        else:
            values = after(arrived, *values)
        send_q, own, near_part, far_part = values
        from_far.append(far_swap(far_part, n in RELAYED))
        if n == 0:
            first_q = swap(send_q)
        sends.append(send_q)
        nears.append(near_part)
        owns.append(own)
    from_near.append(near_swap(nears[-1]))
    for n in range(max(count - 2, 0), count):
        finish(n)
    for n in range(max(count - 2, 0), count):
        out_q, *out_kv = place(side, kv_parts[n], (out_q, *out_kv), arrivals(n))
    return (out_q, *out_kv)


def solution(mesh):
    placed = P("ctx", "section")
    out = P(("ctx", "section"), None)
    return jax.shard_map(
        on_device,
        mesh=mesh,
        in_specs=(placed, placed, placed, placed, P()),
        out_specs=(out, out, out),
        check_vma=False,
    )
```

```python
import functools
import math

import jax
import jax.numpy as jnp
from jax import lax
from jax.experimental import pallas as pl
from jax.experimental.pallas import tpu as pltpu
from jax.sharding import PartitionSpec as P

HEAD = 128
H = 20
TILE = 128
ROWS = 256
CHUNKS = (6, 7, 7)
RELAYED = (1,)
SCALE = 1.0 / math.sqrt(HEAD)
LOG2E = math.log2(math.e)
DEAD = -1e30
BF16 = jnp.bfloat16
COST = pl.CostEstimate(flops=1000, transcendentals=0, bytes_accessed=1000)
PARAMS = pltpu.CompilerParams(vmem_limit_bytes=67_000_000)

NT = (((1,), (1,)), ((), ()))
NN = (((1,), (0,)), ((), ()))
TN = (((0,), (0,)), ((), ()))


def dot(a, b, dims):
    return lax.dot_general(a, b, dims, preferred_element_type=jnp.float32)


def split_rows(side, rows, keep_ref, send_ref):
    @pl.when(side == 0)
    def _():
        keep_ref[...] = rows[:TILE]
        send_ref[...] = rows[TILE:]

    @pl.when(side == 1)
    def _():
        keep_ref[...] = rows[TILE:]
        send_ref[...] = rows[:TILE]


def attn_kernel(
    side_ref, q_ref, do_ref, k_ref, v_ref, nk_ref, nv_ref, far_ref, bias_ref, *refs
):
    keep_ref, send_ref, own_ref, near_out, far_out = refs[-5:]
    q, do = q_ref[...], do_ref[...]
    groups = [
        (nk_ref[...], nv_ref[...], near_out),
        (k_ref[...], v_ref[...], own_ref),
        (far_ref[0], far_ref[1], far_out),
    ]
    ts, tops = [], []
    for g, (kg, _, _) in enumerate(groups):
        s = dot(kg, q, NT) * (SCALE * LOG2E)
        for half in range(2):
            t = s[half * TILE : (half + 1) * TILE] + bias_ref[2 * g + half : 2 * g + half + 1, :]
            ts.append(t)
            tops.append(jnp.max(t, axis=0, keepdims=True))
    top = functools.reduce(jnp.maximum, tops)
    es = [jnp.exp2(t - top) for t in ts]
    total = sum(jnp.sum(e, axis=0, keepdims=True) for e in es)
    dps, acc = [], 0.0
    for g, (_, vg, _) in enumerate(groups):
        dp = dot(vg, do, NT)
        for half in range(2):
            d = dp[half * TILE : (half + 1) * TILE]
            dps.append(d)
            acc = acc + jnp.sum(es[2 * g + half] * d, axis=0, keepdims=True)
    inv = 1.0 / total
    delta = acc * inv
    inv_scaled = inv * SCALE
    dq = None
    for g, (kg, _, out) in enumerate(groups):
        pair = (2 * g, 2 * g + 1)
        w = jnp.concatenate([(es[j] * inv).astype(BF16) for j in pair], axis=0)
        ds = jnp.concatenate(
            [((es[j] * inv_scaled) * (dps[j] - delta)).astype(BF16) for j in pair], axis=0
        )
        out[0] = dot(ds, q, NN).astype(BF16)
        out[1] = dot(w, do, NN).astype(BF16)
        part = dot(ds, kg, TN)
        dq = part if dq is None else dq + part
    split_rows(side_ref[0], dq.astype(BF16), keep_ref, send_ref)


def attn_chunk(side, q, do, k, v, near_k, near_v, far, bias, out, h0, hc):
    block = pl.BlockSpec((ROWS, HEAD), lambda i, s: (0, h0 + i))
    pair = pl.BlockSpec((2, ROWS, HEAD), lambda i, s: (0, 0, i))
    specs = [block] * 6 + [pair, pl.BlockSpec((8, ROWS), lambda i, s: (0, 0))]
    args, alias = [q, do, k, v, near_k, near_v, far, bias], {}
    if out is not None:
        specs.append(pl.BlockSpec(memory_space=pl.ANY))
        args.append(out)
        alias = {9: 0}
    return pl.pallas_call(
        attn_kernel,
        grid_spec=pltpu.PrefetchScalarGridSpec(
            num_scalar_prefetch=1,
            grid=(hc,),
            in_specs=specs,
            out_specs=[
                pl.BlockSpec((TILE, HEAD), lambda i, s: (0, s[0] * H + h0 + i)),
                pl.BlockSpec((TILE, HEAD), lambda i, s: (0, i)),
                pair,
                pair,
                pair,
            ],
        ),
        out_shape=[
            pltpu.HBM((TILE, 2 * H * HEAD), BF16),
            pltpu.HBM((TILE, hc * HEAD), BF16),
        ]
        + [pltpu.HBM((2, ROWS, hc * HEAD), BF16)] * 3,
        input_output_aliases=alias,
        compiler_params=PARAMS,
        cost_estimate=COST,
        name="attn",
    )(side, *args)


def columns(side, h0, hc):
    return pl.ds(pl.multiple_of(side * (H * HEAD) + h0 * HEAD, HEAD), hc * HEAD)


def run_all(copies):
    for copy in copies:
        copy.start()
    for copy in copies:
        copy.wait()


def combine_kernel(h0, hc, relayed, extra, moves, n_in, side_ref, corner_ref, *refs):
    f32, side = jnp.float32, side_ref[0]
    ins, outs = refs[:n_in], refs[n_in : n_in + 4]
    parts, kept, sent, in_sems, out_sems, carry_sems, *stages = refs[n_in + 4 :]
    keep_k, keep_v, send_ref, out_q = outs
    fetches = [
        [
            pltpu.make_async_copy(ins[n].at[j], parts.at[j, n], in_sems.at[j, n])
            for n in range(3 + relayed)
        ]
        for j in range(2)
    ]
    carries, at = [], 3 + relayed
    if extra:
        carries.append((ins[at], send_ref.at[pl.ds(2 * TILE, TILE), pl.ds(0, extra * HEAD)]))
        at += 1
    for part, row, out, o0, oc in moves:
        source = ins[at + part].at[pl.ds(row, TILE), pl.ds(0, oc * HEAD)]
        carries.append((source, (out_q, keep_k, keep_v)[out].at[:, columns(1 - side, o0, oc)]))
    carries = [
        (
            pltpu.make_async_copy(source, stages[n], carry_sems.at[n, 0]),
            pltpu.make_async_copy(stages[n], target, carry_sems.at[n, 1]),
        )
        for n, (source, target) in enumerate(carries)
    ]
    for copy in fetches[0] + fetches[1] + [fetch for fetch, _ in carries]:
        copy.start()
    leaving = []
    for j, keep in enumerate((keep_k, keep_v)):
        for copy in fetches[j]:
            copy.wait()
        far = parts[j, 2]
        if relayed:
            far = jnp.where(corner_ref[0] == 1, parts[j, 3], far)
        total = parts[j, 0].astype(f32) + parts[j, 1].astype(f32) + far.astype(f32)
        split_rows(side, total.astype(BF16), kept.at[j], sent.at[j])
        leaving += [
            pltpu.make_async_copy(
                sent.at[j],
                send_ref.at[pl.ds(j * TILE, TILE), pl.ds(0, hc * HEAD)],
                out_sems.at[j, 0],
            ),
            pltpu.make_async_copy(
                kept.at[j], keep.at[:, columns(side, h0, hc)], out_sems.at[j, 1]
            ),
        ]
        for copy in leaving[-2:]:
            copy.start()
    for fetch, store in carries:
        fetch.wait()
        store.start()
        leaving.append(store)
    for copy in leaving:
        copy.wait()


def combine(side, corner, own, from_near, from_far, out_q, out_kv, send_q, extra, arrived, moves, h0, hc):
    width, relayed = hc * HEAD, len(from_far) - 1
    anywhere = pl.BlockSpec(memory_space=pl.ANY)
    args = [own, from_near, *from_far, *([send_q] if extra else []), *arrived]
    alias = {2 + len(args): 3}
    args.append(out_q)
    if out_kv is not None:
        alias |= {2 + len(args): 0, 3 + len(args): 1}
        args += list(out_kv)
    send_shape = (3 * TILE, max(hc, extra) * HEAD) if extra else (2 * TILE, width)
    stages = ([(TILE, extra * HEAD)] if extra else []) + [(TILE, m[4] * HEAD) for m in moves]
    whole = pltpu.HBM((TILE, 2 * H * HEAD), BF16)
    return pl.pallas_call(
        functools.partial(combine_kernel, h0, hc, relayed, extra, moves, len(args)),
        grid_spec=pltpu.PrefetchScalarGridSpec(
            num_scalar_prefetch=2,
            grid=(1,),
            in_specs=[anywhere] * len(args),
            out_specs=[anywhere] * 4,
            scratch_shapes=[
                pltpu.VMEM((2, 3 + relayed, ROWS, width), BF16),
                pltpu.VMEM((2, TILE, width), BF16),
                pltpu.VMEM((2, TILE, width), BF16),
                pltpu.SemaphoreType.DMA((2, 3 + relayed)),
                pltpu.SemaphoreType.DMA((2, 2)),
                pltpu.SemaphoreType.DMA((max(len(stages), 1), 2)),
            ]
            + [pltpu.VMEM(shape, BF16) for shape in stages],
        ),
        out_shape=[whole, whole, pltpu.HBM(send_shape, BF16), whole],
        input_output_aliases=alias,
        compiler_params=PARAMS,
        cost_estimate=COST,
        name="combine",
    )(side, corner, *args)


def place_kernel(moves, side_ref, *refs):
    sems = refs[-1]
    outs = refs[-4:-1]
    run_all(
        [
            pltpu.make_async_copy(
                refs[0].at[pl.ds(row, TILE), pl.ds(0, oc * HEAD)],
                outs[out].at[:, columns(1 - side_ref[0], o0, oc)],
                sems.at[n],
            )
            for n, (row, out, o0, oc) in enumerate(moves)
        ]
    )


def place(side, part, outs, moves):
    anywhere = pl.BlockSpec(memory_space=pl.ANY)
    return pl.pallas_call(
        functools.partial(place_kernel, moves),
        grid_spec=pltpu.PrefetchScalarGridSpec(
            num_scalar_prefetch=1,
            grid=(1,),
            in_specs=[pl.BlockSpec(part.shape, lambda i, s: (0, 0))] + [anywhere] * 3,
            out_specs=[anywhere] * 3,
            scratch_shapes=[pltpu.SemaphoreType.DMA((len(moves),))],
        ),
        out_shape=[pltpu.HBM((TILE, 2 * H * HEAD), BF16)] * 3,
        input_output_aliases={2 + j: j for j in range(3)},
        compiler_params=PARAMS,
        cost_estimate=COST,
        name="place",
    )(side, part, *outs)


def pack_kernel(spans, k_ref, v_ref, *refs):
    count = len(spans)
    outs, stages, sems = refs[:count], refs[count : 2 * count], refs[-1]
    moves = []
    for n, (h0, hc) in enumerate(spans):
        for j, src in enumerate((k_ref, v_ref)):
            cols = pl.ds(h0 * HEAD, hc * HEAD)
            moves.append(
                (
                    pltpu.make_async_copy(src.at[:, cols], stages[n].at[j], sems.at[n, j, 0]),
                    pltpu.make_async_copy(stages[n].at[j], outs[n].at[j], sems.at[n, j, 1]),
                )
            )
    for fetch, _ in moves:
        fetch.start()
    for fetch, store in moves:
        fetch.wait()
        store.start()
    for _, store in moves:
        store.wait()


def pack(k, v, spans):
    return pl.pallas_call(
        functools.partial(pack_kernel, spans),
        grid=(1,),
        in_specs=[pl.BlockSpec(memory_space=pl.ANY)] * 2,
        out_specs=[pl.BlockSpec(memory_space=pl.ANY)] * len(spans),
        out_shape=[pltpu.HBM((2, ROWS, hc * HEAD), BF16) for _, hc in spans],
        scratch_shapes=[pltpu.VMEM((2, ROWS, hc * HEAD), BF16) for _, hc in spans]
        + [pltpu.SemaphoreType.DMA((len(spans), 2, 2))],
        compiler_params=PARAMS,
        cost_estimate=COST,
        name="pack",
    )(k, v)


def near_swap(x):
    return lax.ppermute(x, "ctx", [(i, i ^ 1) for i in range(lax.axis_size("ctx"))])


def corners():
    count = lax.axis_size("ctx")
    return (0, count // 2 - 1, count // 2, count - 1)


def far_pairs():
    count = lax.axis_size("ctx")
    return [(i, (i + 2 * (i % 2) - 1) % count) for i in range(count)]


def far_swap(x, in_legs=False):
    half = lax.axis_size("ctx") // 2
    pairs = [(i, j ^ half if in_legs and i in corners() else j) for i, j in far_pairs()]
    return lax.ppermute(x, "ctx", pairs)


def across_x(x):
    half = lax.axis_size("ctx") // 2
    return lax.ppermute(x, "ctx", [(i, i ^ half) for i in corners()])


def swap(x):
    return lax.ppermute(x, "section", [(0, 1), (1, 0)])


def split_heads(sizes):
    return [(sum(sizes[:n]), size) for n, size in enumerate(sizes)]


def on_device(queries, key_states, value_states, out_grad, tile_mask):
    position = lax.axis_index("ctx")
    at_corner = functools.reduce(jnp.logical_or, [position == i for i in corners()])
    at_corner = at_corner.astype(jnp.int32).reshape(1)
    side = lax.axis_index("section").astype(jnp.int32).reshape(1)
    own_mask = lax.dynamic_slice_in_dim(tile_mask, position * 2, 2, 0)
    bias = jnp.where(jnp.repeat(own_mask.T, TILE, axis=1) > 0, 0.0, DEAD).astype(jnp.float32)
    before, own, after = bias[0:2], bias[2:4], bias[4:6]
    odd = position % 2 == 1
    near = jnp.where(odd, before, after)
    far = jnp.where(odd, after, before)
    bias = jnp.concatenate([near, own, far, jnp.zeros((2, ROWS), jnp.float32)], axis=0)

    spans = split_heads(CHUNKS)
    count = len(spans)
    near_k, near_v = near_swap(key_states), near_swap(value_states)
    packs = list(pack(key_states, value_states, spans[:1]))
    later_keys, near_k = lax.optimization_barrier((key_states, near_k))
    packs += pack(later_keys, value_states, spans[1:])
    fars = [far_swap(x) for x in packs]
    bias, *_ = lax.optimization_barrier((bias, *packs))

    out_q, out_kv = None, None
    sends, kv_parts, owns, from_far, from_near = [], [], [], [], []
    first_q = None

    def arrivals(n):
        moves = [(0, 1, *spans[n]), (TILE, 2, *spans[n])]
        return moves + ([(2 * TILE, 0, *spans[n + 1])] if n + 1 < count else [])

    def finish(n):
        nonlocal out_q, out_kv
        legs = [from_far[n]]
        if n in RELAYED:
            (first_leg,) = after([(owns, n + 1)], from_far[n])
            legs.append(across_x(first_leg))
        last = n + 1 == count
        arrived, moves = [], []
        if n == 1:
            arrived, moves = [first_q], [(0, 0, 0, *spans[0])]
        if n >= 2:
            arrived, moves = [kv_parts[n - 2]], [(0, *move) for move in arrivals(n - 2)]
        *out_kv, send, out_q = combine(
            side, at_corner, owns[n], from_near[n], legs, out_q, out_kv,
            None if last else sends[n + 1], 0 if last else spans[n + 1][1], arrived, moves, *spans[n],
        )
        kv_parts.append(swap(send))

    def after(arrived, *values):
        held = lax.optimization_barrier((*values, *(where[i] for where, i in arrived)))
        for (where, i), value in zip(arrived, held[len(values) :]):
            where[i] = value
        return held[: len(values)]

    nears = []
    for n, (h0, hc) in enumerate(spans):
        if n >= 1:
            arrived = [(fars, n)] + ([(from_far, n - 2)] if n >= 2 else [])
            (near_part,) = after(arrived, nears[n - 1])
            from_near.append(near_swap(near_part))
            if n >= 2:
                finish(n - 2)
                fars[n], out_kv[0] = lax.optimization_barrier((fars[n], out_kv[0]))
        out_q, send_q, own, near_part, far_part = attn_chunk(
            side, queries, out_grad, key_states, value_states, near_k, near_v, fars[n], bias,
            out_q, h0, hc,
        )
        arrived = [(from_near, n - 1)] if n >= 1 else []
        if n >= 1 and n + 1 < count:
            arrived.append((fars, n + 1))
        values = (send_q, own, near_part, far_part)
        if n == 1:
            *values, first_q = after(arrived, *values, first_q)
        else:
            values = after(arrived, *values)
        send_q, own, near_part, far_part = values
        if n >= 2:
            (near_part,) = after([(kv_parts, n - 2)], near_part)
        from_far.append(far_swap(far_part, n in RELAYED))
        if n == 0:
            first_q = swap(send_q)
        sends.append(send_q)
        nears.append(near_part)
        owns.append(own)
    from_near.append(near_swap(nears[-1]))
    for n in range(max(count - 2, 0), count):
        finish(n)
    for n in range(max(count - 2, 0), count):
        out_q, *out_kv = place(side, kv_parts[n], (out_q, *out_kv), arrivals(n))
    return (out_q, *out_kv)


def solution(mesh):
    placed = P("ctx", "section")
    out = P(("ctx", "section"), None)
    return jax.shard_map(
        on_device,
        mesh=mesh,
        in_specs=(placed, placed, placed, placed, P()),
        out_specs=(out, out, out),
        check_vma=False,
    )
```

```python
import functools
import math

import jax
import jax.numpy as jnp
from jax import lax
from jax.experimental import pallas as pl
from jax.experimental.pallas import tpu as pltpu
from jax.sharding import PartitionSpec as P

HEAD = 128
H = 20
TILE = 128
ROWS = 256
CHUNKS = (6, 7, 7)
RELAYED = (1,)
SCALE = 1.0 / math.sqrt(HEAD)
LOG2E = math.log2(math.e)
DEAD = -1e30
BF16 = jnp.bfloat16
COST = pl.CostEstimate(flops=1000, transcendentals=0, bytes_accessed=1000)
PARAMS = pltpu.CompilerParams(vmem_limit_bytes=67_000_000)

NT = (((1,), (1,)), ((), ()))
NN = (((1,), (0,)), ((), ()))
TN = (((0,), (0,)), ((), ()))


def dot(a, b, dims):
    return lax.dot_general(a, b, dims, preferred_element_type=jnp.float32)


def split_rows(side, rows, keep_ref, send_ref):
    @pl.when(side == 0)
    def _():
        keep_ref[...] = rows[:TILE]
        send_ref[...] = rows[TILE:]

    @pl.when(side == 1)
    def _():
        keep_ref[...] = rows[TILE:]
        send_ref[...] = rows[:TILE]


def attn_kernel(
    side_ref, q_ref, do_ref, k_ref, v_ref, nk_ref, nv_ref, far_ref, bias_ref, *refs
):
    keep_ref, send_ref, own_ref, near_out, far_out = refs[-5:]
    q, do = q_ref[...], do_ref[...]
    groups = [
        (nk_ref[...], nv_ref[...], near_out),
        (k_ref[...], v_ref[...], own_ref),
        (far_ref[0], far_ref[1], far_out),
    ]
    ts, tops = [], []
    for g, (kg, _, _) in enumerate(groups):
        s = dot(kg, q, NT) * (SCALE * LOG2E)
        for half in range(2):
            t = s[half * TILE : (half + 1) * TILE] + bias_ref[2 * g + half : 2 * g + half + 1, :]
            ts.append(t)
            tops.append(jnp.max(t, axis=0, keepdims=True))
    top = functools.reduce(jnp.maximum, tops)
    es = [jnp.exp2(t - top) for t in ts]
    total = sum(jnp.sum(e, axis=0, keepdims=True) for e in es)
    dps, acc = [], 0.0
    for g, (_, vg, _) in enumerate(groups):
        dp = dot(vg, do, NT)
        for half in range(2):
            d = dp[half * TILE : (half + 1) * TILE]
            dps.append(d)
            acc = acc + jnp.sum(es[2 * g + half] * d, axis=0, keepdims=True)
    inv = 1.0 / total
    delta = acc * inv
    inv_scaled = inv * SCALE
    dq = None
    for g, (kg, _, out) in enumerate(groups):
        pair = (2 * g, 2 * g + 1)
        w = jnp.concatenate([(es[j] * inv).astype(BF16) for j in pair], axis=0)
        ds = jnp.concatenate(
            [((es[j] * inv_scaled) * (dps[j] - delta)).astype(BF16) for j in pair], axis=0
        )
        out[0] = dot(ds, q, NN).astype(BF16)
        out[1] = dot(w, do, NN).astype(BF16)
        part = dot(ds, kg, TN)
        dq = part if dq is None else dq + part
    split_rows(side_ref[0], dq.astype(BF16), keep_ref, send_ref)


def attn_chunk(side, q, do, k, v, near_k, near_v, far, bias, out, h0, hc):
    block = pl.BlockSpec((ROWS, HEAD), lambda i, s: (0, h0 + i))
    pair = pl.BlockSpec((2, ROWS, HEAD), lambda i, s: (0, 0, i))
    specs = [block] * 6 + [pair, pl.BlockSpec((8, ROWS), lambda i, s: (0, 0))]
    args, alias = [q, do, k, v, near_k, near_v, far, bias], {}
    if out is not None:
        specs.append(pl.BlockSpec(memory_space=pl.ANY))
        args.append(out)
        alias = {9: 0}
    return pl.pallas_call(
        attn_kernel,
        grid_spec=pltpu.PrefetchScalarGridSpec(
            num_scalar_prefetch=1,
            grid=(hc,),
            in_specs=specs,
            out_specs=[
                pl.BlockSpec((TILE, HEAD), lambda i, s: (0, s[0] * H + h0 + i)),
                pl.BlockSpec((TILE, HEAD), lambda i, s: (0, i)),
                pair,
                pair,
                pair,
            ],
        ),
        out_shape=[
            pltpu.HBM((TILE, 2 * H * HEAD), BF16),
            pltpu.HBM((TILE, hc * HEAD), BF16),
        ]
        + [pltpu.HBM((2, ROWS, hc * HEAD), BF16)] * 3,
        input_output_aliases=alias,
        compiler_params=PARAMS,
        cost_estimate=COST,
        name="attn",
    )(side, *args)


def columns(side, h0, hc):
    return pl.ds(pl.multiple_of(side * (H * HEAD) + h0 * HEAD, HEAD), hc * HEAD)


def run_all(copies):
    for copy in copies:
        copy.start()
    for copy in copies:
        copy.wait()


def combine_kernel(h0, hc, relayed, extra, moves, n_in, side_ref, corner_ref, *refs):
    f32, side = jnp.float32, side_ref[0]
    ins, outs = refs[:n_in], refs[n_in : n_in + 4]
    parts, kept, sent, in_sems, out_sems, carry_sems, *stages = refs[n_in + 4 :]
    keep_k, keep_v, send_ref, out_q = outs
    fetches = [
        [
            pltpu.make_async_copy(ins[n].at[j], parts.at[j, n], in_sems.at[j, n])
            for n in range(3 + relayed)
        ]
        for j in range(2)
    ]
    carries, at = [], 3 + relayed
    if extra:
        carries.append((ins[at], send_ref.at[pl.ds(2 * TILE, TILE), pl.ds(0, extra * HEAD)]))
        at += 1
    for part, row, out, o0, oc in moves:
        source = ins[at + part].at[pl.ds(row, TILE), pl.ds(0, oc * HEAD)]
        carries.append((source, (out_q, keep_k, keep_v)[out].at[:, columns(1 - side, o0, oc)]))
    carries = [
        (
            pltpu.make_async_copy(source, stages[n], carry_sems.at[n, 0]),
            pltpu.make_async_copy(stages[n], target, carry_sems.at[n, 1]),
        )
        for n, (source, target) in enumerate(carries)
    ]
    for copy in fetches[0] + fetches[1] + [fetch for fetch, _ in carries]:
        copy.start()
    leaving = []
    for j, keep in enumerate((keep_k, keep_v)):
        for copy in fetches[j]:
            copy.wait()
        far = parts[j, 2]
        if relayed:
            far = jnp.where(corner_ref[0] == 1, parts[j, 3], far)
        total = parts[j, 0].astype(f32) + parts[j, 1].astype(f32) + far.astype(f32)
        split_rows(side, total.astype(BF16), kept.at[j], sent.at[j])
        leaving += [
            pltpu.make_async_copy(
                sent.at[j],
                send_ref.at[pl.ds(j * TILE, TILE), pl.ds(0, hc * HEAD)],
                out_sems.at[j, 0],
            ),
            pltpu.make_async_copy(
                kept.at[j], keep.at[:, columns(side, h0, hc)], out_sems.at[j, 1]
            ),
        ]
        for copy in leaving[-2:]:
            copy.start()
    for fetch, store in carries:
        fetch.wait()
        store.start()
        leaving.append(store)
    for copy in leaving:
        copy.wait()


def combine(side, corner, own, from_near, from_far, out_q, out_kv, send_q, extra, arrived, moves, h0, hc):
    width, relayed = hc * HEAD, len(from_far) - 1
    anywhere = pl.BlockSpec(memory_space=pl.ANY)
    args = [own, from_near, *from_far, *([send_q] if extra else []), *arrived]
    alias = {2 + len(args): 3}
    args.append(out_q)
    if out_kv is not None:
        alias |= {2 + len(args): 0, 3 + len(args): 1}
        args += list(out_kv)
    send_shape = (3 * TILE, max(hc, extra) * HEAD) if extra else (2 * TILE, width)
    stages = ([(TILE, extra * HEAD)] if extra else []) + [(TILE, m[4] * HEAD) for m in moves]
    whole = pltpu.HBM((TILE, 2 * H * HEAD), BF16)
    return pl.pallas_call(
        functools.partial(combine_kernel, h0, hc, relayed, extra, moves, len(args)),
        grid_spec=pltpu.PrefetchScalarGridSpec(
            num_scalar_prefetch=2,
            grid=(1,),
            in_specs=[anywhere] * len(args),
            out_specs=[anywhere] * 4,
            scratch_shapes=[
                pltpu.VMEM((2, 3 + relayed, ROWS, width), BF16),
                pltpu.VMEM((2, TILE, width), BF16),
                pltpu.VMEM((2, TILE, width), BF16),
                pltpu.SemaphoreType.DMA((2, 3 + relayed)),
                pltpu.SemaphoreType.DMA((2, 2)),
                pltpu.SemaphoreType.DMA((max(len(stages), 1), 2)),
            ]
            + [pltpu.VMEM(shape, BF16) for shape in stages],
        ),
        out_shape=[whole, whole, pltpu.HBM(send_shape, BF16), whole],
        input_output_aliases=alias,
        compiler_params=PARAMS,
        cost_estimate=COST,
        name="combine",
    )(side, corner, *args)


def place_kernel(moves, side_ref, *refs):
    sems = refs[-1]
    outs = refs[-4:-1]
    run_all(
        [
            pltpu.make_async_copy(
                refs[0].at[pl.ds(row, TILE), pl.ds(0, oc * HEAD)],
                outs[out].at[:, columns(1 - side_ref[0], o0, oc)],
                sems.at[n],
            )
            for n, (row, out, o0, oc) in enumerate(moves)
        ]
    )


def place(side, part, outs, moves):
    anywhere = pl.BlockSpec(memory_space=pl.ANY)
    return pl.pallas_call(
        functools.partial(place_kernel, moves),
        grid_spec=pltpu.PrefetchScalarGridSpec(
            num_scalar_prefetch=1,
            grid=(1,),
            in_specs=[pl.BlockSpec(part.shape, lambda i, s: (0, 0))] + [anywhere] * 3,
            out_specs=[anywhere] * 3,
            scratch_shapes=[pltpu.SemaphoreType.DMA((len(moves),))],
        ),
        out_shape=[pltpu.HBM((TILE, 2 * H * HEAD), BF16)] * 3,
        input_output_aliases={2 + j: j for j in range(3)},
        compiler_params=PARAMS,
        cost_estimate=COST,
        name="place",
    )(side, part, *outs)


def pack_kernel(spans, k_ref, v_ref, *refs):
    count = len(spans)
    outs, stages, sems = refs[:count], refs[count : 2 * count], refs[-1]
    moves = []
    for n, (h0, hc) in enumerate(spans):
        for j, src in enumerate((k_ref, v_ref)):
            cols = pl.ds(h0 * HEAD, hc * HEAD)
            moves.append(
                (
                    pltpu.make_async_copy(src.at[:, cols], stages[n].at[j], sems.at[n, j, 0]),
                    pltpu.make_async_copy(stages[n].at[j], outs[n].at[j], sems.at[n, j, 1]),
                )
            )
    for fetch, _ in moves:
        fetch.start()
    for fetch, store in moves:
        fetch.wait()
        store.start()
    for _, store in moves:
        store.wait()


def pack(k, v, spans):
    return pl.pallas_call(
        functools.partial(pack_kernel, spans),
        grid=(1,),
        in_specs=[pl.BlockSpec(memory_space=pl.ANY)] * 2,
        out_specs=[pl.BlockSpec(memory_space=pl.ANY)] * len(spans),
        out_shape=[pltpu.HBM((2, ROWS, hc * HEAD), BF16) for _, hc in spans],
        scratch_shapes=[pltpu.VMEM((2, ROWS, hc * HEAD), BF16) for _, hc in spans]
        + [pltpu.SemaphoreType.DMA((len(spans), 2, 2))],
        compiler_params=PARAMS,
        cost_estimate=COST,
        name="pack",
    )(k, v)


def near_swap(x):
    return lax.ppermute(x, "ctx", [(i, i ^ 1) for i in range(lax.axis_size("ctx"))])


def corners():
    count = lax.axis_size("ctx")
    return (0, count // 2 - 1, count // 2, count - 1)


def far_pairs():
    count = lax.axis_size("ctx")
    return [(i, (i + 2 * (i % 2) - 1) % count) for i in range(count)]


def far_swap(x, in_legs=False):
    half = lax.axis_size("ctx") // 2
    pairs = [(i, j ^ half if in_legs and i in corners() else j) for i, j in far_pairs()]
    return lax.ppermute(x, "ctx", pairs)


def across_x(x):
    half = lax.axis_size("ctx") // 2
    return lax.ppermute(x, "ctx", [(i, i ^ half) for i in corners()])


def swap(x):
    return lax.ppermute(x, "section", [(0, 1), (1, 0)])


def split_heads(sizes):
    return [(sum(sizes[:n]), size) for n, size in enumerate(sizes)]


def on_device(queries, key_states, value_states, out_grad, tile_mask):
    position = lax.axis_index("ctx")
    at_corner = functools.reduce(jnp.logical_or, [position == i for i in corners()])
    at_corner = at_corner.astype(jnp.int32).reshape(1)
    side = lax.axis_index("section").astype(jnp.int32).reshape(1)
    own_mask = lax.dynamic_slice_in_dim(tile_mask, position * 2, 2, 0)
    bias = jnp.where(jnp.repeat(own_mask.T, TILE, axis=1) > 0, 0.0, DEAD).astype(jnp.float32)
    before, own, after = bias[0:2], bias[2:4], bias[4:6]
    odd = position % 2 == 1
    near = jnp.where(odd, before, after)
    far = jnp.where(odd, after, before)
    bias = jnp.concatenate([near, own, far, jnp.zeros((2, ROWS), jnp.float32)], axis=0)

    spans = split_heads(CHUNKS)
    count = len(spans)
    near_k, near_v = near_swap(key_states), near_swap(value_states)
    packs = list(pack(key_states, value_states, spans[:1]))
    later_keys, near_k = lax.optimization_barrier((key_states, near_k))
    packs += pack(later_keys, value_states, spans[1:])
    fars = [far_swap(x) for x in packs]
    bias, *_ = lax.optimization_barrier((bias, *packs))

    out_q, out_kv = None, None
    sends, kv_parts, owns, from_far, from_near = [], [], [], [], []
    first_q = None

    def arrivals(n):
        moves = [(0, 1, *spans[n]), (TILE, 2, *spans[n])]
        return moves + ([(2 * TILE, 0, *spans[n + 1])] if n + 2 < count else [])

    def finish(n):
        nonlocal out_q, out_kv
        legs = [from_far[n]]
        if n in RELAYED:
            (first_leg,) = after([(owns, n + 1)], from_far[n])
            legs.append(across_x(first_leg))
        rides = n + 2 < count
        arrived, moves = [], []
        if n == 1:
            arrived, moves = [first_q], [(0, 0, 0, *spans[0])]
        if n >= 2:
            arrived, moves = [kv_parts[n - 2]], [(0, *move) for move in arrivals(n - 2)]
        if n + 1 == count:
            arrived.append(last_q)
            moves.append((len(arrived) - 1, 0, 0, *spans[n]))
        *out_kv, send, out_q = combine(
            side, at_corner, owns[n], from_near[n], legs, out_q, out_kv,
            sends[n + 1] if rides else None, spans[n + 1][1] if rides else 0, arrived, moves, *spans[n],
        )
        kv_parts.append(swap(send))

    def after(arrived, *values):
        held = lax.optimization_barrier((*values, *(where[i] for where, i in arrived)))
        for (where, i), value in zip(arrived, held[len(values) :]):
            where[i] = value
        return held[: len(values)]

    nears = []
    for n, (h0, hc) in enumerate(spans):
        if n >= 1:
            arrived = [(fars, n)] + ([(from_far, n - 2)] if n >= 2 else [])
            (near_part,) = after(arrived, nears[n - 1])
            from_near.append(near_swap(near_part))
            if n >= 2:
                finish(n - 2)
                fars[n], out_kv[0] = lax.optimization_barrier((fars[n], out_kv[0]))
        out_q, send_q, own, near_part, far_part = attn_chunk(
            side, queries, out_grad, key_states, value_states, near_k, near_v, fars[n], bias,
            out_q, h0, hc,
        )
        arrived = [(from_near, n - 1)] if n >= 1 else []
        if n >= 1 and n + 1 < count:
            arrived.append((fars, n + 1))
        values = (send_q, own, near_part, far_part)
        if n == 1:
            *values, first_q = after(arrived, *values, first_q)
        else:
            values = after(arrived, *values)
        send_q, own, near_part, far_part = values
        if n >= 2:
            (near_part,) = after([(kv_parts, n - 2)], near_part)
        from_far.append(far_swap(far_part, n in RELAYED))
        if n == 0:
            first_q = swap(send_q)
        if n + 1 == count:
            last_q = swap(send_q)
        sends.append(send_q)
        nears.append(near_part)
        owns.append(own)
    from_near.append(near_swap(nears[-1]))
    for n in range(max(count - 2, 0), count):
        finish(n)
    for n in range(max(count - 2, 0), count):
        out_q, *out_kv = place(side, kv_parts[n], (out_q, *out_kv), arrivals(n))
    return (out_q, *out_kv)


def solution(mesh):
    placed = P("ctx", "section")
    out = P(("ctx", "section"), None)
    return jax.shard_map(
        on_device,
        mesh=mesh,
        in_specs=(placed, placed, placed, placed, P()),
        out_specs=(out, out, out),
        check_vma=False,
    )
```

```python
import functools
import math

import jax
import jax.numpy as jnp
from jax import lax
from jax.experimental import pallas as pl
from jax.experimental.pallas import tpu as pltpu
from jax.sharding import PartitionSpec as P

HEAD = 128
H = 20
TILE = 128
ROWS = 256
CHUNKS = (6, 7, 7)
RELAYED = (1,)
SCALE = 1.0 / math.sqrt(HEAD)
LOG2E = math.log2(math.e)
DEAD = -1e30
BF16 = jnp.bfloat16
COST = pl.CostEstimate(flops=1000, transcendentals=0, bytes_accessed=1000)
PARAMS = pltpu.CompilerParams(vmem_limit_bytes=67_000_000)

NT = (((1,), (1,)), ((), ()))
NN = (((1,), (0,)), ((), ()))
TN = (((0,), (0,)), ((), ()))


def dot(a, b, dims):
    return lax.dot_general(a, b, dims, preferred_element_type=jnp.float32)


def split_rows(side, rows, keep_ref, send_ref):
    @pl.when(side == 0)
    def _():
        keep_ref[...] = rows[:TILE]
        send_ref[...] = rows[TILE:]

    @pl.when(side == 1)
    def _():
        keep_ref[...] = rows[TILE:]
        send_ref[...] = rows[:TILE]


def attn_kernel(
    side_ref, q_ref, do_ref, k_ref, v_ref, nk_ref, nv_ref, far_ref, bias_ref, *refs
):
    keep_ref, send_ref, own_ref, near_out, far_out = refs[-5:]
    q, do = q_ref[...], do_ref[...]
    groups = [
        (nk_ref[...], nv_ref[...], near_out),
        (k_ref[...], v_ref[...], own_ref),
        (far_ref[0], far_ref[1], far_out),
    ]
    ts, tops = [], []
    for g, (kg, _, _) in enumerate(groups):
        s = dot(kg, q, NT) * (SCALE * LOG2E)
        for half in range(2):
            t = s[half * TILE : (half + 1) * TILE] + bias_ref[2 * g + half : 2 * g + half + 1, :]
            ts.append(t)
            tops.append(jnp.max(t, axis=0, keepdims=True))
    top = functools.reduce(jnp.maximum, tops)
    es = [jnp.exp2(t - top) for t in ts]
    total = sum(jnp.sum(e, axis=0, keepdims=True) for e in es)
    dps, acc = [], 0.0
    for g, (_, vg, _) in enumerate(groups):
        dp = dot(vg, do, NT)
        for half in range(2):
            d = dp[half * TILE : (half + 1) * TILE]
            dps.append(d)
            acc = acc + jnp.sum(es[2 * g + half] * d, axis=0, keepdims=True)
    inv = 1.0 / total
    delta = acc * inv
    inv_scaled = inv * SCALE
    dq = None
    for g, (kg, _, out) in enumerate(groups):
        pair = (2 * g, 2 * g + 1)
        w = jnp.concatenate([(es[j] * inv).astype(BF16) for j in pair], axis=0)
        ds = jnp.concatenate(
            [((es[j] * inv_scaled) * (dps[j] - delta)).astype(BF16) for j in pair], axis=0
        )
        out[0] = dot(ds, q, NN).astype(BF16)
        out[1] = dot(w, do, NN).astype(BF16)
        part = dot(ds, kg, TN)
        dq = part if dq is None else dq + part
    split_rows(side_ref[0], dq.astype(BF16), keep_ref, send_ref)


def attn_chunk(side, q, do, k, v, near_k, near_v, far, bias, out, h0, hc):
    block = pl.BlockSpec((ROWS, HEAD), lambda i, s: (0, h0 + i))
    pair = pl.BlockSpec((2, ROWS, HEAD), lambda i, s: (0, 0, i))
    specs = [block] * 6 + [pair, pl.BlockSpec((8, ROWS), lambda i, s: (0, 0))]
    args, alias = [q, do, k, v, near_k, near_v, far, bias], {}
    if out is not None:
        specs.append(pl.BlockSpec(memory_space=pl.ANY))
        args.append(out)
        alias = {9: 0}
    return pl.pallas_call(
        attn_kernel,
        grid_spec=pltpu.PrefetchScalarGridSpec(
            num_scalar_prefetch=1,
            grid=(hc,),
            in_specs=specs,
            out_specs=[
                pl.BlockSpec((TILE, HEAD), lambda i, s: (0, s[0] * H + h0 + i)),
                pl.BlockSpec((TILE, HEAD), lambda i, s: (0, i)),
                pair,
                pair,
                pair,
            ],
        ),
        out_shape=[
            pltpu.HBM((TILE, 2 * H * HEAD), BF16),
            pltpu.HBM((TILE, hc * HEAD), BF16),
        ]
        + [pltpu.HBM((2, ROWS, hc * HEAD), BF16)] * 3,
        input_output_aliases=alias,
        compiler_params=PARAMS,
        cost_estimate=COST,
        name="attn",
    )(side, *args)


def columns(side, h0, hc):
    return pl.ds(pl.multiple_of(side * (H * HEAD) + h0 * HEAD, HEAD), hc * HEAD)


def run_all(copies):
    for copy in copies:
        copy.start()
    for copy in copies:
        copy.wait()


def combine_kernel(h0, hc, relayed, extra, moves, n_in, side_ref, corner_ref, *refs):
    f32, side = jnp.float32, side_ref[0]
    ins, outs = refs[:n_in], refs[n_in : n_in + 4]
    parts, kept, sent, in_sems, out_sems, carry_sems, *stages = refs[n_in + 4 :]
    keep_k, keep_v, send_ref, out_q = outs
    fetches = [
        [
            pltpu.make_async_copy(ins[n].at[j], parts.at[j, n], in_sems.at[j, n])
            for n in range(3)
        ]
        for j in range(2)
    ]
    carries, at = [], 3 + relayed
    if extra:
        carries.append((ins[at], send_ref.at[pl.ds(2 * TILE, TILE), pl.ds(0, extra * HEAD)]))
        at += 1
    for part, row, out, o0, oc in moves:
        source = ins[at + part].at[pl.ds(row, TILE), pl.ds(0, oc * HEAD)]
        carries.append((source, (out_q, keep_k, keep_v)[out].at[:, columns(1 - side, o0, oc)]))
    carries = [
        (
            pltpu.make_async_copy(source, stages[n], carry_sems.at[n, 0]),
            pltpu.make_async_copy(stages[n], target, carry_sems.at[n, 1]),
        )
        for n, (source, target) in enumerate(carries)
    ]
    if relayed:
        at_corner = corner_ref[0] == 1
        for j in range(2):
            straight = fetches[j][2]
            across = pltpu.make_async_copy(ins[3].at[j], parts.at[j, 2], in_sems.at[j, 2])
            pl.when(at_corner)(across.start)
            pl.when(jnp.logical_not(at_corner))(straight.start)
    for j in range(2):
        for copy in fetches[j][: 2 if relayed else 3]:
            copy.start()
    for fetch, _ in carries:
        fetch.start()
    leaving = []
    for j, keep in enumerate((keep_k, keep_v)):
        for copy in fetches[j]:
            copy.wait()
        total = parts[j, 0].astype(f32) + parts[j, 1].astype(f32) + parts[j, 2].astype(f32)
        split_rows(side, total.astype(BF16), kept.at[j], sent.at[j])
        leaving += [
            pltpu.make_async_copy(
                sent.at[j],
                send_ref.at[pl.ds(j * TILE, TILE), pl.ds(0, hc * HEAD)],
                out_sems.at[j, 0],
            ),
            pltpu.make_async_copy(
                kept.at[j], keep.at[:, columns(side, h0, hc)], out_sems.at[j, 1]
            ),
        ]
        for copy in leaving[-2:]:
            copy.start()
    for fetch, store in carries:
        fetch.wait()
        store.start()
        leaving.append(store)
    for copy in leaving:
        copy.wait()


def combine(side, corner, own, from_near, from_far, out_q, out_kv, send_q, extra, arrived, moves, h0, hc):
    width, relayed = hc * HEAD, len(from_far) - 1
    anywhere = pl.BlockSpec(memory_space=pl.ANY)
    args = [own, from_near, *from_far, *([send_q] if extra else []), *arrived]
    alias = {2 + len(args): 3}
    args.append(out_q)
    if out_kv is not None:
        alias |= {2 + len(args): 0, 3 + len(args): 1}
        args += list(out_kv)
    send_shape = (3 * TILE, max(hc, extra) * HEAD) if extra else (2 * TILE, width)
    stages = ([(TILE, extra * HEAD)] if extra else []) + [(TILE, m[4] * HEAD) for m in moves]
    whole = pltpu.HBM((TILE, 2 * H * HEAD), BF16)
    return pl.pallas_call(
        functools.partial(combine_kernel, h0, hc, relayed, extra, moves, len(args)),
        grid_spec=pltpu.PrefetchScalarGridSpec(
            num_scalar_prefetch=2,
            grid=(1,),
            in_specs=[anywhere] * len(args),
            out_specs=[anywhere] * 4,
            scratch_shapes=[
                pltpu.VMEM((2, 3, ROWS, width), BF16),
                pltpu.VMEM((2, TILE, width), BF16),
                pltpu.VMEM((2, TILE, width), BF16),
                pltpu.SemaphoreType.DMA((2, 3)),
                pltpu.SemaphoreType.DMA((2, 2)),
                pltpu.SemaphoreType.DMA((max(len(stages), 1), 2)),
            ]
            + [pltpu.VMEM(shape, BF16) for shape in stages],
        ),
        out_shape=[whole, whole, pltpu.HBM(send_shape, BF16), whole],
        input_output_aliases=alias,
        compiler_params=PARAMS,
        cost_estimate=COST,
        name="combine",
    )(side, corner, *args)


def place_kernel(moves, side_ref, *refs):
    sems = refs[-1]
    outs = refs[-4:-1]
    run_all(
        [
            pltpu.make_async_copy(
                refs[0].at[pl.ds(row, TILE), pl.ds(0, oc * HEAD)],
                outs[out].at[:, columns(1 - side_ref[0], o0, oc)],
                sems.at[n],
            )
            for n, (row, out, o0, oc) in enumerate(moves)
        ]
    )


def place(side, part, outs, moves):
    anywhere = pl.BlockSpec(memory_space=pl.ANY)
    return pl.pallas_call(
        functools.partial(place_kernel, moves),
        grid_spec=pltpu.PrefetchScalarGridSpec(
            num_scalar_prefetch=1,
            grid=(1,),
            in_specs=[pl.BlockSpec(part.shape, lambda i, s: (0, 0))] + [anywhere] * 3,
            out_specs=[anywhere] * 3,
            scratch_shapes=[pltpu.SemaphoreType.DMA((len(moves),))],
        ),
        out_shape=[pltpu.HBM((TILE, 2 * H * HEAD), BF16)] * 3,
        input_output_aliases={2 + j: j for j in range(3)},
        compiler_params=PARAMS,
        cost_estimate=COST,
        name="place",
    )(side, part, *outs)


def pack_kernel(spans, k_ref, v_ref, *refs):
    count = len(spans)
    outs, stages, sems = refs[:count], refs[count : 2 * count], refs[-1]
    moves = []
    for n, (h0, hc) in enumerate(spans):
        for j, src in enumerate((k_ref, v_ref)):
            cols = pl.ds(h0 * HEAD, hc * HEAD)
            moves.append(
                (
                    pltpu.make_async_copy(src.at[:, cols], stages[n].at[j], sems.at[n, j, 0]),
                    pltpu.make_async_copy(stages[n].at[j], outs[n].at[j], sems.at[n, j, 1]),
                )
            )
    for fetch, _ in moves:
        fetch.start()
    for fetch, store in moves:
        fetch.wait()
        store.start()
    for _, store in moves:
        store.wait()


def pack(k, v, spans):
    return pl.pallas_call(
        functools.partial(pack_kernel, spans),
        grid=(1,),
        in_specs=[pl.BlockSpec(memory_space=pl.ANY)] * 2,
        out_specs=[pl.BlockSpec(memory_space=pl.ANY)] * len(spans),
        out_shape=[pltpu.HBM((2, ROWS, hc * HEAD), BF16) for _, hc in spans],
        scratch_shapes=[pltpu.VMEM((2, ROWS, hc * HEAD), BF16) for _, hc in spans]
        + [pltpu.SemaphoreType.DMA((len(spans), 2, 2))],
        compiler_params=PARAMS,
        cost_estimate=COST,
        name="pack",
    )(k, v)


def near_swap(x):
    return lax.ppermute(x, "ctx", [(i, i ^ 1) for i in range(lax.axis_size("ctx"))])


def corners():
    count = lax.axis_size("ctx")
    return (0, count // 2 - 1, count // 2, count - 1)


def far_pairs():
    count = lax.axis_size("ctx")
    return [(i, (i + 2 * (i % 2) - 1) % count) for i in range(count)]


def far_swap(x, in_legs=False):
    half = lax.axis_size("ctx") // 2
    pairs = [(i, j ^ half if in_legs and i in corners() else j) for i, j in far_pairs()]
    return lax.ppermute(x, "ctx", pairs)


def across_x(x):
    half = lax.axis_size("ctx") // 2
    return lax.ppermute(x, "ctx", [(i, i ^ half) for i in corners()])


def swap(x):
    return lax.ppermute(x, "section", [(0, 1), (1, 0)])


def split_heads(sizes):
    return [(sum(sizes[:n]), size) for n, size in enumerate(sizes)]


def on_device(queries, key_states, value_states, out_grad, tile_mask):
    position = lax.axis_index("ctx")
    at_corner = functools.reduce(jnp.logical_or, [position == i for i in corners()])
    at_corner = at_corner.astype(jnp.int32).reshape(1)
    side = lax.axis_index("section").astype(jnp.int32).reshape(1)
    own_mask = lax.dynamic_slice_in_dim(tile_mask, position * 2, 2, 0)
    bias = jnp.where(jnp.repeat(own_mask.T, TILE, axis=1) > 0, 0.0, DEAD).astype(jnp.float32)
    before, own, after = bias[0:2], bias[2:4], bias[4:6]
    odd = position % 2 == 1
    near = jnp.where(odd, before, after)
    far = jnp.where(odd, after, before)
    bias = jnp.concatenate([near, own, far, jnp.zeros((2, ROWS), jnp.float32)], axis=0)

    spans = split_heads(CHUNKS)
    count = len(spans)
    near_k, near_v = near_swap(key_states), near_swap(value_states)
    packs = list(pack(key_states, value_states, spans[:1]))
    later_keys, near_k = lax.optimization_barrier((key_states, near_k))
    packs += pack(later_keys, value_states, spans[1:])
    fars = [far_swap(x) for x in packs]
    bias, *_ = lax.optimization_barrier((bias, *packs))

    out_q, out_kv = None, None
    sends, kv_parts, owns, from_far, from_near = [], [], [], [], []
    first_q = None

    def arrivals(n):
        moves = [(0, 1, *spans[n]), (TILE, 2, *spans[n])]
        return moves + ([(2 * TILE, 0, *spans[n + 1])] if n + 2 < count else [])

    def finish(n):
        nonlocal out_q, out_kv
        legs = [from_far[n]]
        if n in RELAYED:
            (first_leg,) = after([(owns, n + 1)], from_far[n])
            legs.append(across_x(first_leg))
        rides = n + 2 < count
        arrived, moves = [], []
        if n == 1:
            arrived, moves = [first_q], [(0, 0, 0, *spans[0])]
        if n >= 2:
            arrived, moves = [kv_parts[n - 2]], [(0, *move) for move in arrivals(n - 2)]
        if n + 1 == count:
            arrived.append(last_q)
            moves.append((len(arrived) - 1, 0, 0, *spans[n]))
        *out_kv, send, out_q = combine(
            side, at_corner, owns[n], from_near[n], legs, out_q, out_kv,
            sends[n + 1] if rides else None, spans[n + 1][1] if rides else 0, arrived, moves, *spans[n],
        )
        kv_parts.append(swap(send))

    def after(arrived, *values):
        held = lax.optimization_barrier((*values, *(where[i] for where, i in arrived)))
        for (where, i), value in zip(arrived, held[len(values) :]):
            where[i] = value
        return held[: len(values)]

    nears = []
    for n, (h0, hc) in enumerate(spans):
        if n >= 1:
            arrived = [(fars, n)] + ([(from_far, n - 2)] if n >= 2 else [])
            (near_part,) = after(arrived, nears[n - 1])
            from_near.append(near_swap(near_part))
            if n >= 2:
                finish(n - 2)
                fars[n], out_kv[0] = lax.optimization_barrier((fars[n], out_kv[0]))
        out_q, send_q, own, near_part, far_part = attn_chunk(
            side, queries, out_grad, key_states, value_states, near_k, near_v, fars[n], bias,
            out_q, h0, hc,
        )
        arrived = [(from_near, n - 1)] if n >= 1 else []
        if n >= 1 and n + 1 < count:
            arrived.append((fars, n + 1))
        values = (send_q, own, near_part, far_part)
        if n == 1:
            *values, first_q = after(arrived, *values, first_q)
        else:
            values = after(arrived, *values)
        send_q, own, near_part, far_part = values
        if n >= 2:
            (near_part,) = after([(kv_parts, n - 2)], near_part)
        from_far.append(far_swap(far_part, n in RELAYED))
        if n == 0:
            first_q = swap(send_q)
        if n + 1 == count:
            last_q = swap(send_q)
        sends.append(send_q)
        nears.append(near_part)
        owns.append(own)
    from_near.append(near_swap(nears[-1]))
    for n in range(max(count - 2, 0), count):
        finish(n)
    for n in range(max(count - 2, 0), count):
        out_q, *out_kv = place(side, kv_parts[n], (out_q, *out_kv), arrivals(n))
    return (out_q, *out_kv)


def solution(mesh):
    placed = P("ctx", "section")
    out = P(("ctx", "section"), None)
    return jax.shard_map(
        on_device,
        mesh=mesh,
        in_specs=(placed, placed, placed, placed, P()),
        out_specs=(out, out, out),
        check_vma=False,
    )
```
